32 devices in a mesh: dp: 2 (over core), row: 4 (over y, x), col: 4 (over z).
Axes of the slice: x: 2, y: 2, z: 4, core: 2. Of those that a mesh axis runs over, the one named last changes fastest.
Arguments:
- tokens: bfloat16 [1024, 768], P(('dp', 'col'), 'row'), may hold values from -150 to 150
- out_grad: bfloat16 [1024, 768], P(('dp', 'col'), 'row'), may hold values from -6 to 6
- segment_ids: int32 [2, 512], P('dp'), may hold values from 0 to 1, never falling along the last dimension, each value on 1 to 384 neighbouring positions
- w_qkv: bfloat16 [768, 2304], P('row', 'col'), may hold values from -8 to 8
- w_out: bfloat16 [768, 768], P('col', 'row'), may hold values from -0.875 to 0.875
- w_fc: bfloat16 [768, 3072], P('row', 'col'), may hold values from -0.21875 to 0.21875
- w_proj: bfloat16 [3072, 768], P('col', 'row'), may hold values from -0.109375 to 0.109375
- bias_qkv: float32 [2304], P('col'), may hold values from -1.8 to 1.8
- bias_fc: float32 [3072], P('col'), may hold values from -1.8 to 1.8
- row_vectors: float32 [6, 768], P(None, 'row'), may hold values from -0.6 to 1.5
- mom_qkv: float32 [768, 2304], P('row', 'col'), may hold values from -20 to 20
- mom_out: float32 [768, 768], P('col', 'row'), may hold values from -20 to 20
- mom_fc: float32 [768, 3072], P('row', 'col'), may hold values from -20 to 20
- mom_proj: float32 [3072, 768], P('col', 'row'), may hold values from -20 to 20
- mom_bias_qkv: float32 [2304], P('col'), may hold values from -20 to 20
- mom_bias_fc: float32 [3072], P('col'), may hold values from -20 to 20
- mom_rows: float32 [6, 768], P(None, 'row'), may hold values from -20 to 20
Outputs:
- block_out: bfloat16 [1024, 768], P(('dp', 'col'), 'row')
- input_grad: float32 [1024, 768], P(('dp', 'col'), 'row')
- grad_qkv: float32 [768, 2304], P('row', 'col')
- grad_out: float32 [768, 768], P('col', 'row')
- grad_fc: float32 [768, 3072], P('row', 'col')
- grad_proj: float32 [3072, 768], P('col', 'row')
- grad_bias_qkv: float32 [2304], P('col')
- grad_bias_fc: float32 [3072], P('col')
- grad_rows: float32 [6, 768], P(None, 'row')
- new_qkv: float32 [768, 2304], P('row', 'col')
- new_out: float32 [768, 768], P('col', 'row')
- new_fc: float32 [768, 3072], P('row', 'col')
- new_proj: float32 [3072, 768], P('col', 'row')
- new_bias_qkv: float32 [2304], P('col')
- new_bias_fc: float32 [3072], P('col')
- new_rows: float32 [6, 768], P(None, 'row')
- new_mom_qkv: float32 [768, 2304], P('row', 'col')
- new_mom_out: float32 [768, 768], P('col', 'row')
- new_mom_fc: float32 [768, 3072], P('row', 'col')
- new_mom_proj: float32 [3072, 768], P('col', 'row')
- new_mom_bias_qkv: float32 [2304], P('col')
- new_mom_bias_fc: float32 [3072], P('col')
- new_mom_rows: float32 [6, 768], P(None, 'row')
The draws below stay inside these ranges and needn't reach their ends.
Inputs may be any that keep to these rules, and one draw needn't show every extreme that they name: `segment_ids`: within each data group the segment numbers never fall; the group's 2 sequences have 512 tokens together, each at most 384.
All inputs are finite; a program needn't handle non-finite values.
Results may differ from the reference program's by a relative error of at most 0.012.
Values may be sent and summed in bfloat16 or wider, within the bound.
A program may use at most 128 MiB of HBM per device.

```python
import math
import jax
import jax.numpy as jnp
import numpy as np
from jax import lax

D = 768
HEADS = 12
HD = 64
FF = 3072
TOK_G = 512
NS_STEPS = 2
SEGS = 2
GROUPS = 2
TOKENS = 1024
LONGEST = 384


def draw_tokens(key, part):
    sub_keys = jax.random.split(key, 3)
    rising = 3.0 ** (jnp.arange(D, dtype=jnp.float32) / D)
    spread = jnp.exp(jax.random.uniform(sub_keys[1], (D,), jnp.float32, 0.0, math.log(10.0)))
    column = rising * spread / 5.0
    offset = jnp.clip(jax.random.normal(sub_keys[2], (D,), jnp.float32), -2.0, 2.0) * 0.5
    base = jnp.clip(jax.random.normal(sub_keys[0], (TOKENS, D), jnp.float32), -4.0, 4.0)
    return ((base + offset) * column).astype(jnp.bfloat16)


def draw_w_qkv(key, part):
    sub_keys = jax.random.split(key, 1)
    base = jnp.clip(jax.random.normal(sub_keys[0], (D, HEADS, 3, HD), jnp.float32), -4.0, 4.0) / math.sqrt(D)
    return base.reshape(D, 3 * D).astype(jnp.bfloat16)


def draw_row_vectors(key, part):
    sub_keys = jax.random.split(key, 2)
    gains = jax.random.uniform(sub_keys[0], (6, D), jnp.float32, 0.5, 1.5)
    shifts = jnp.clip(jax.random.normal(sub_keys[1], (6, D), jnp.float32), -3.0, 3.0) * 0.2
    which_rows = jnp.arange(6, dtype=jnp.int32)
    picked = (which_rows % 2 == 0) & (which_rows < 4)
    return jnp.where(picked[:, None], gains, shifts)


def block_scale(own_key, shape, cuts, least, largest):
    level, own = 1.0, jax.random.fold_in(own_key, 6)
    for position, blocks in cuts:
        steps = jnp.exp(jax.random.uniform(jax.random.fold_in(own, position), (blocks,), jnp.float32, least / len(cuts), largest / len(cuts)))
        level = level * jnp.repeat(steps, shape[position] // blocks).reshape([-1 if axis == position else 1 for axis in range(len(shape))])
    return level


def length_profile(count, total, most, skew):
    portions = [(1 << 20) // math.isqrt(rank ** skew) + 1 for rank in range(2, count + 1)]
    rest, counts = total - most - (count - 1), [1] * (count - 1)
    while rest > 0:
        free = [i for i in range(count - 1) if counts[i] < most]
        mass, remaining = sum([portions[i] for i in free]), rest
        for i in free:
            extra = min(most - counts[i], max(1, remaining * portions[i] // mass), rest)
            counts[i] = counts[i] + extra
            rest = rest - extra
    return np.array([most] + counts)


def uneven_parts(own_key, number_of, total, limit, lean):
    if number_of == 2:
        one = jax.random.randint(own_key, (), max(1, total - limit), min(limit, total - 1) + 1)
        return jnp.stack([one, total - one])
    sizes = jnp.asarray(length_profile(number_of, total, limit, lean), jnp.int32)
    couples = (number_of - 1) // 2
    source_of, taker = sizes[1:1 + 2 * couples:2], sizes[2:2 + 2 * couples:2]
    slack = jnp.minimum(source_of - 1, limit - taker)
    passed = jax.random.randint(jax.random.fold_in(own_key, 1), (couples,), 0, 1 << 20) % (slack + 1)
    sizes = sizes.at[1:1 + 2 * couples:2].set(source_of - passed).at[2:2 + 2 * couples:2].set(taker + passed)
    return sizes[jax.random.permutation(jax.random.fold_in(own_key, 2), number_of)]


def noise(stream_key, dims, scale, bound, shards=(), kind=jnp.bfloat16):
    gain = block_scale(stream_key, dims, shards, -0.22, 0.18) if shards else 1.0
    result = jax.random.normal(stream_key, dims, jnp.float32) * scale * gain
    return jnp.minimum(jnp.maximum(result, -bound), bound).astype(kind)


def setup_inputs(seed: int = 0) -> dict:
    splits = jax.random.split(jax.random.key(seed), 18)
    return {
        "tokens": draw_tokens(jax.random.fold_in(splits[17], 71), 0),
        "out_grad": noise(splits[1], (TOKENS, D), 1.0, 6.0, ((0, 8), (1, 4))),
        "segment_ids": jax.vmap(lambda own: jnp.searchsorted(jnp.cumsum(uneven_parts(own, SEGS, TOK_G, LONGEST, 2)), jnp.arange(TOK_G), side="right"))(jax.random.split(splits[2], GROUPS)).reshape((GROUPS, TOK_G)).astype(jnp.int32),
        "w_qkv": draw_w_qkv(jax.random.fold_in(splits[17], 71), 0),
        "w_out": noise(splits[4], (D, D), (D // 16) ** -0.5, 0.875, ((0, 4), (1, 4))),
        "w_fc": noise(splits[5], (D, FF), D ** -0.5, 0.21875, ((0, 4), (1, 4))),
        "w_proj": noise(splits[6], (FF, D), FF ** -0.5, 0.109375, ((0, 4), (1, 4))),
        "bias_qkv": noise(splits[7], (3 * D,), 0.3, 1.8, ((0, 4),), jnp.float32),
        "bias_fc": noise(splits[8], (FF,), 0.3, 1.8, ((0, 4),), jnp.float32),
        "row_vectors": draw_row_vectors(jax.random.fold_in(splits[17], 71), 0),
        "mom_qkv": noise(splits[10], (D, 3 * D), (0.1 * TOKENS ** 0.5), 20.0, ((0, 4), (1, 4)), jnp.float32),
        "mom_out": noise(splits[11], (D, D), (0.1 * TOKENS ** 0.5), 20.0, ((0, 4), (1, 4)), jnp.float32),
        "mom_fc": noise(splits[12], (D, FF), (0.1 * TOKENS ** 0.5), 20.0, ((0, 4), (1, 4)), jnp.float32),
        "mom_proj": noise(splits[13], (FF, D), (0.1 * TOKENS ** 0.5), 20.0, ((0, 4), (1, 4)), jnp.float32),
        "mom_bias_qkv": noise(splits[14], (3 * D,), (0.1 * TOKENS ** 0.5), 20.0, ((0, 4),), jnp.float32),
        "mom_bias_fc": noise(splits[15], (FF,), (0.1 * TOKENS ** 0.5), 20.0, ((0, 4),), jnp.float32),
        "mom_rows": noise(splits[16], (6, D), (0.1 * TOKENS ** 0.5), 20.0, ((1, 4),), jnp.float32),
    }


eps_norm = 1e-05
eps_gram = 1e-06
coef_a = 3.4445
coef_b = -4.775
coef_c = 2.0315
beta_mom = 0.95
rate_matrix = 0.03
rate_vector = 0.6

def round_low(values):
    return lax.optimization_barrier(values.astype(jnp.bfloat16)).astype(jnp.float32)

def gelu_value(values):
    return jax.nn.gelu(values, approximate=True)

def gelu_slope(values):
    return jax.vjp(gelu_value, values)[1](jnp.ones_like(values))[0]

def norm_forward(values, gain_row, shift_row):
    mean_row = lax.optimization_barrier(jnp.mean(values, axis=1, keepdims=True))
    square = lax.optimization_barrier(jnp.mean(values * values, axis=1, keepdims=True))
    inv_std = lax.rsqrt(square - mean_row * mean_row + eps_norm)
    unit_rows = (values - mean_row) * inv_std
    return (unit_rows, inv_std, unit_rows * gain_row + shift_row)

def norm_backward(grad_rows, unit_rows, inv_std, gain_row):
    scaled = grad_rows * gain_row
    first_mean = lax.optimization_barrier(jnp.mean(scaled, axis=1, keepdims=True))
    second_mean = lax.optimization_barrier(jnp.mean(scaled * unit_rows, axis=1, keepdims=True))
    return inv_std * (scaled - first_mean - unit_rows * second_mean)

def wide_einsum(form, left_side, right_side):
    return jnp.einsum(form, left_side.astype(jnp.float32), right_side.astype(jnp.float32), precision=lax.Precision.HIGHEST)

def attend_forward(query_rows, key_rows, value_rows, allowed, score_scale):
    scores = wide_einsum('qhe,khe->hqk', query_rows, key_rows) * score_scale
    scores = jnp.where(allowed[None], scores, -jnp.inf)
    row_max = lax.optimization_barrier(jnp.max(scores, axis=2, keepdims=True))
    log_total = row_max + jnp.log(lax.optimization_barrier(jnp.sum(jnp.exp(scores - row_max), axis=2, keepdims=True)))
    prob_low = round_low(jnp.exp(scores - log_total))
    attended = wide_einsum('hqk,khe->qhe', prob_low, value_rows)
    return (attended.astype(jnp.bfloat16), log_total)

def attend_grad(query_rows, key_rows, value_rows, allowed, score_scale, grad_low, attended, log_total):
    scores = wide_einsum('qhe,khe->hqk', query_rows, key_rows) * score_scale
    scores = jnp.where(allowed[None], scores, -jnp.inf)
    probs_full = jnp.exp(scores - log_total)
    prob_low = round_low(probs_full)
    grad_value = wide_einsum('hqk,qhe->khe', prob_low, grad_low)
    grad_probs = wide_einsum('qhe,khe->hqk', grad_low, value_rows)
    row_dot = lax.optimization_barrier(jnp.sum(grad_low.astype(jnp.float32) * attended.astype(jnp.float32), axis=2)).T[:, :, None]
    grad_scores = round_low(score_scale * probs_full * (grad_probs - row_dot))
    grad_query = wide_einsum('hqk,khe->qhe', grad_scores, key_rows)
    grad_key = wide_einsum('hqk,qhe->khe', grad_scores, query_rows)
    return (grad_query, grad_key, grad_value)

def orthogonalize(update_low):
    flipped = update_low.shape[0] > update_low.shape[1]
    matrix = update_low.T if flipped else update_low
    gram_matrix = jnp.dot(matrix, matrix.T, preferred_element_type=jnp.float32)
    gram_norm = jnp.sqrt(jnp.sum(gram_matrix * gram_matrix)) + eps_gram
    current = (matrix.astype(jnp.float32) / jnp.sqrt(gram_norm)).astype(jnp.bfloat16)
    gram_low = (gram_matrix / gram_norm).astype(jnp.bfloat16)
    for repeat in range(NS_STEPS):
        if repeat > 0:
            gram_low = jnp.dot(current, current.T, preferred_element_type=jnp.float32).astype(jnp.bfloat16)
        polynomial = (coef_b * gram_low.astype(jnp.float32) + coef_c * jnp.dot(gram_low, gram_low, preferred_element_type=jnp.float32)).astype(jnp.bfloat16)
        current = (coef_a * current.astype(jnp.float32) + jnp.dot(polynomial, current, preferred_element_type=jnp.float32)).astype(jnp.bfloat16)
    return current.T if flipped else current

def reference(tokens, out_grad, segment_ids, w_qkv, w_out, w_fc, w_proj, bias_qkv, bias_fc, row_vectors, mom_qkv, mom_out, mom_fc, mom_proj, mom_bias_qkv, mom_bias_fc, mom_rows):
    score_scale = 1.0 / math.sqrt(HD)
    gain_one = row_vectors[0]
    shift_one = row_vectors[1]
    gain_two = row_vectors[2]
    shift_two = row_vectors[3]
    bias_out = row_vectors[4]
    bias_proj = row_vectors[5]
    positions = jnp.arange(TOK_G, dtype=jnp.int32)

    def group_pass(carry, inputs):
        tok_group, grad_group, seg_group = inputs
        resid_in = tok_group.astype(jnp.float32)
        unit_one, inv_one, normed_one = norm_forward(resid_in, gain_one, shift_one)
        act_one = normed_one.astype(jnp.bfloat16)
        qkv_all = (jnp.dot(act_one, w_qkv, preferred_element_type=jnp.float32) + bias_qkv).astype(jnp.bfloat16)
        qkv_tiles = qkv_all.reshape(TOK_G, HEADS, 3, HD)
        query_rows = qkv_tiles[:, :, 0]
        key_rows = qkv_tiles[:, :, 1]
        value_rows = qkv_tiles[:, :, 2]
        allowed = (positions[None, :] <= positions[:, None]) & (seg_group[None, :] == seg_group[:, None])
        attended, log_total = attend_forward(query_rows, key_rows, value_rows, allowed, score_scale)
        attn_flat = attended.reshape(TOK_G, D)
        resid_mid = resid_in + jnp.dot(attn_flat, w_out, preferred_element_type=jnp.float32) + bias_out
        unit_two, inv_two, normed_two = norm_forward(resid_mid, gain_two, shift_two)
        act_two = normed_two.astype(jnp.bfloat16)
        hidden_pre = jnp.dot(act_two, w_fc, preferred_element_type=jnp.float32) + bias_fc
        hidden = gelu_value(hidden_pre).astype(jnp.bfloat16)
        block_out = (resid_mid + jnp.dot(hidden, w_proj, preferred_element_type=jnp.float32) + bias_proj).astype(jnp.bfloat16)
        grad_hidden = jnp.dot(grad_group, w_proj.T, preferred_element_type=jnp.float32)
        grad_pre = (gelu_slope(hidden_pre) * grad_hidden).astype(jnp.bfloat16)
        grad_w_proj = jnp.dot(hidden.T, grad_group, preferred_element_type=jnp.float32)
        grad_w_fc = jnp.dot(act_two.T, grad_pre, preferred_element_type=jnp.float32)
        grad_b_fc = lax.optimization_barrier(jnp.sum(grad_pre.astype(jnp.float32), axis=0))
        grad_norm_two = jnp.dot(grad_pre, w_fc.T, preferred_element_type=jnp.float32)
        grad_mid = grad_group.astype(jnp.float32) + norm_backward(grad_norm_two, unit_two, inv_two, gain_two)
        grad_mid_low = grad_mid.astype(jnp.bfloat16)
        grad_w_out = jnp.dot(attn_flat.T, grad_mid_low, preferred_element_type=jnp.float32)
        grad_attn = jnp.dot(grad_mid_low, w_out.T, preferred_element_type=jnp.float32).astype(jnp.bfloat16)
        grad_query, grad_key, grad_value = attend_grad(query_rows, key_rows, value_rows, allowed, score_scale, grad_attn.reshape(TOK_G, HEADS, HD), attended, log_total)
        grad_qkv = jnp.stack([grad_query, grad_key, grad_value], axis=2).reshape(TOK_G, 3 * D).astype(jnp.bfloat16)
        grad_w_qkv = jnp.dot(act_one.T, grad_qkv, preferred_element_type=jnp.float32)
        grad_b_qkv = lax.optimization_barrier(jnp.sum(grad_qkv.astype(jnp.float32), axis=0))
        grad_norm_one = jnp.dot(grad_qkv, w_qkv.T, preferred_element_type=jnp.float32)
        input_grad = grad_mid + norm_backward(grad_norm_one, unit_one, inv_one, gain_one)
        row_terms = jnp.stack([lax.optimization_barrier(jnp.sum(grad_norm_one * unit_one, axis=0)), lax.optimization_barrier(jnp.sum(grad_norm_one, axis=0)), lax.optimization_barrier(jnp.sum(grad_norm_two * unit_two, axis=0)), lax.optimization_barrier(jnp.sum(grad_norm_two, axis=0)), lax.optimization_barrier(jnp.sum(grad_mid_low.astype(jnp.float32), axis=0)), lax.optimization_barrier(jnp.sum(grad_group.astype(jnp.float32), axis=0))])
        terms = (grad_w_qkv, grad_w_out, grad_w_fc, grad_w_proj, grad_b_qkv, grad_b_fc, row_terms)
        new_carry = tuple((previous + current for previous, current in zip(carry, terms)))
        return (new_carry, (block_out, input_grad))
    start_carry = (jnp.zeros((D, 3 * D), jnp.float32), jnp.zeros((D, D), jnp.float32), jnp.zeros((D, FF), jnp.float32), jnp.zeros((FF, D), jnp.float32), jnp.zeros((3 * D,), jnp.float32), jnp.zeros((FF,), jnp.float32), jnp.zeros((6, D), jnp.float32))
    sums, outputs = lax.scan(group_pass, start_carry, (tokens.reshape(GROUPS, TOK_G, D), out_grad.reshape(GROUPS, TOK_G, D), segment_ids))
    block_out = outputs[0].reshape(TOKENS, D)
    input_grad = outputs[1].reshape(TOKENS, D)

    def matrix_step(weight, gradient, moment):
        new_moment = beta_mom * moment + gradient
        pushed = (gradient + beta_mom * new_moment).astype(jnp.bfloat16)
        ortho = orthogonalize(pushed)
        factor = rate_matrix * math.sqrt(max(weight.shape[0], weight.shape[1]))
        return (weight.astype(jnp.float32) - factor * ortho.astype(jnp.float32), new_moment)

    def vector_step(weight, gradient, moment):
        new_moment = beta_mom * moment + gradient
        return (weight - rate_vector / math.sqrt(TOKENS) * (gradient + beta_mom * new_moment), new_moment)
    new_qkv, new_mom_qkv = matrix_step(w_qkv, sums[0], mom_qkv)
    new_out, new_mom_out = matrix_step(w_out, sums[1], mom_out)
    new_fc, new_mom_fc = matrix_step(w_fc, sums[2], mom_fc)
    new_proj, new_mom_proj = matrix_step(w_proj, sums[3], mom_proj)
    new_bias_qkv, new_mom_bias_qkv = vector_step(bias_qkv, sums[4], mom_bias_qkv)
    new_bias_fc, new_mom_bias_fc = vector_step(bias_fc, sums[5], mom_bias_fc)
    new_rows, new_mom_rows = vector_step(row_vectors, sums[6], mom_rows)
    return (block_out, input_grad, sums[0], sums[1], sums[2], sums[3], sums[4], sums[5], sums[6], new_qkv, new_out, new_fc, new_proj, new_bias_qkv, new_bias_fc, new_rows, new_mom_qkv, new_mom_out, new_mom_fc, new_mom_proj, new_mom_bias_qkv, new_mom_bias_fc, new_mom_rows)
```

```python
import functools
import math

import jax
import jax.numpy as jnp
from jax import lax
from jax.experimental import pallas as pl
from jax.experimental.pallas import tpu as pltpu
from jax.sharding import PartitionSpec as P

HD = 64
NS_STEPS = 2


eps_norm = 1e-05
eps_gram = 1e-06
coef_a = 3.4445
coef_b = -4.775
coef_c = 2.0315
beta_mom = 0.95
rate_matrix = 0.03
rate_vector = 0.6


def gelu_value(values):
    return jax.nn.gelu(values, approximate=True)


def gelu_slope(values):
    return jax.vjp(gelu_value, values)[1](jnp.ones_like(values))[0]


def product(left_side, right_side, flip_right):
    if flip_right:
        return lax.dot_general(
            left_side, right_side, (((1,), (1,)), ((), ())), preferred_element_type=jnp.float32
        )
    return jnp.dot(left_side, right_side, preferred_element_type=jnp.float32)


def inner_rows(left_side, right_side):
    return lax.dot_general(
        left_side, right_side, (((0,), (0,)), ((), ())), preferred_element_type=jnp.float32
    )


def exchange_kernel(axes, parts, kinds, *refs):
    count = len(kinds)
    sources, targets = refs[:count], refs[count : 2 * count]
    send_sem, recv_sem, local_sem = refs[2 * count :]
    barrier = pltpu.get_barrier_semaphore()
    met = 0
    for axis in sorted(set(axes)):
        axis_parts = parts[axes.index(axis)]
        for step in range(1, axis_parts):
            peer = lax.rem(lax.axis_index(axis) + step, axis_parts)
            pl.semaphore_signal(
                barrier, inc=1, device_id={axis: peer}, device_id_type=pl.DeviceIdType.MESH
            )
            met += 1
    pl.semaphore_wait(barrier, met)
    copies = []
    for which in range(count):
        axis = axes[which]
        me = lax.axis_index(axis)
        for step in range(1, parts[which]):
            peer = lax.rem(me + step, parts[which])
            copy = pltpu.make_async_remote_copy(
                src_ref=sources[which].at[peer] if kinds[which] else sources[which],
                dst_ref=targets[which].at[me],
                send_sem=send_sem.at[which, step - 1],
                recv_sem=recv_sem.at[which, step - 1],
                device_id={axis: peer},
                device_id_type=pl.DeviceIdType.MESH,
            )
            copy.start()
            copies.append(copy)
    for which in range(count):
        me = lax.axis_index(axes[which])
        copy = pltpu.make_async_copy(
            sources[which].at[me] if kinds[which] else sources[which],
            targets[which].at[me],
            local_sem.at[which],
        )
        copy.start()
        copies.append(copy)
    for copy in copies:
        copy.wait()


def exchange(axes, arrays, kinds, name_id):
    count = len(arrays)
    if isinstance(axes, str):
        axes = [axes] * count
    parts = [lax.axis_size(axis) for axis in axes]
    shapes = [
        jax.ShapeDtypeStruct(array.shape if kind else (part,) + array.shape, array.dtype)
        for array, kind, part in zip(arrays, kinds, parts)
    ]
    return pl.pallas_call(
        functools.partial(exchange_kernel, tuple(axes), tuple(parts), tuple(kinds)),
        out_shape=shapes,
        in_specs=[pl.BlockSpec(memory_space=pltpu.VMEM)] * count,
        out_specs=[pl.BlockSpec(memory_space=pltpu.VMEM)] * count,
        scratch_shapes=[
            pltpu.SemaphoreType.DMA((count, max(parts) - 1)),
            pltpu.SemaphoreType.DMA((count, max(parts) - 1)),
            pltpu.SemaphoreType.DMA((count,)),
        ],
        compiler_params=pltpu.CompilerParams(collective_id=name_id, has_side_effects=True),
    )(*arrays)


def total(slots):
    return jnp.sum(slots.astype(jnp.float32), axis=0)


def side_by_side(slots):
    return jnp.concatenate([slots[part] for part in range(slots.shape[0])], axis=1)


def norm_stats(values):
    mean_row = jnp.mean(values, axis=1, keepdims=True)
    square = jnp.mean(values * values, axis=1, keepdims=True)
    inv_std = lax.rsqrt(square - mean_row * mean_row + eps_norm)
    return mean_row, inv_std


def matrix_product(left_side, right_side):
    return jnp.dot(
        left_side.astype(jnp.bfloat16),
        right_side.astype(jnp.bfloat16),
        preferred_element_type=jnp.float32,
    )


def polynomial_factor(gram_matrix):
    gram_norm = jnp.sqrt(jnp.sum(gram_matrix * gram_matrix)) + eps_gram
    gram_now = gram_matrix / gram_norm
    poly_before = None
    for repeat in range(NS_STEPS):
        poly = coef_b * gram_now + coef_c * matrix_product(gram_now, gram_now)
        if poly_before is None:
            factor = poly
            scale = coef_a
        else:
            factor = coef_a * factor + scale * poly + matrix_product(poly, factor)
            scale = scale * coef_a
        if repeat + 1 < NS_STEPS:
            half = coef_a * gram_now + matrix_product(poly, gram_now)
            gram_now = coef_a * half + matrix_product(half, poly)
        poly_before = poly
    return factor, scale, gram_norm


def contract(left_side, right_side, left_dim, right_dim):
    return lax.dot_general(
        left_side,
        right_side,
        (((left_dim,), (right_dim,)), ((), ())),
        preferred_element_type=jnp.float32,
    )


def column_of(row_values):
    size = row_values.shape[1]
    up = lax.broadcasted_iota(jnp.int32, (size, size), 0)
    across = lax.broadcasted_iota(jnp.int32, (size, size), 1)
    return jnp.sum(jnp.where(up == across, row_values, 0.0), axis=1, keepdims=True)


class Wire:
    def __init__(self, send_sem, recv_sem):
        self.send_sem, self.recv_sem = send_sem, recv_sem
        self.used = 0
        self.live = []

    def push(self, source, target, axis, peer):
        copy = pltpu.make_async_remote_copy(
            src_ref=source,
            dst_ref=target,
            send_sem=self.send_sem.at[self.used],
            recv_sem=self.recv_sem.at[self.used],
            device_id={axis: peer},
            device_id_type=pl.DeviceIdType.MESH,
        )
        self.used += 1
        copy.start()
        self.live.append(copy)
        return copy

    def spread(self, axis, source_of, target_of):
        parts = lax.axis_size(axis)
        me = lax.axis_index(axis)
        copies = []
        for step in range(1, parts):
            peer = lax.rem(me + step, parts)
            copies.append(self.push(source_of(peer), target_of(peer), axis, peer))
        return copies

    def drain(self):
        for copy in self.live:
            copy.wait_send()


def greet(axes):
    barrier = pltpu.get_barrier_semaphore()
    met = 0
    for axis in axes:
        parts = lax.axis_size(axis)
        for step in range(1, parts):
            peer = lax.rem(lax.axis_index(axis) + step, parts)
            pl.semaphore_signal(
                barrier, inc=1, device_id={axis: peer}, device_id_type=pl.DeviceIdType.MESH
            )
            met += 1
    pl.semaphore_wait(barrier, met)


def arrived(copies):
    for copy in copies:
        copy.wait_recv()


def rows_at(index, size):
    return pl.ds(pl.multiple_of(index * size, size), size)


front_wires = 110


def front_kernel(*refs):
    low, wide = jnp.bfloat16, jnp.float32
    (
        tok_in, grad_in, seg_row, wq_in, wo_in, wf_in, wp_in, bias_q, bias_f, vec_in,
        sum_q, sum_o, sum_f, sum_p, sum_bq, sum_bf, outward, inward, unit_own, inv_own,
        mid_own, resid_own, wide_out,
        tok, grad_cols, grad_part, vecs, wq, wo, wf, wp, act_one, qkv, bias_col, mask, probs,
        attn, attn_part, unit_two, inv_two, act_two, act_cols, mid, hid, gpre, two_out, two_in,
        gm_piece, mid_part, mid_cols, gattn, gqkv, acc_k, acc_v, mean_one, inv_one,
        send_sem, recv_sem, local_sem,
    ) = refs
    rows, cols = lax.axis_size("row"), lax.axis_size("col")
    me_r, me_c, me_d = lax.axis_index("row"), lax.axis_index("col"), lax.axis_index("dp")
    count, feats = tok.shape[1], tok.shape[2]
    whole = feats * rows
    block = count // cols
    piece = block // cols
    half = feats // 2
    heads = qkv.shape[0] // (3 * HD)
    score_scale = 1.0 / math.sqrt(HD)
    own = rows_at(me_c, block)
    part = rows_at(me_r, block)
    bit = rows_at(me_c, piece)
    wire = Wire(send_sem, recv_sem)
    locals_ = []
    for which, (source, target) in enumerate(
        [
            (tok_in, tok.at[me_r, own]),
            (vec_in, vecs.at[me_r]),
            (wq_in, wq.at[me_r]),
            (grad_in, grad_cols.at[own]),
            (wo_in, wo.at[me_c, me_r]),
            (wf_in, wf.at[me_r]),
            (wp_in, wp.at[me_r]),
        ]
    ):
        copy = pltpu.make_async_copy(source, target, local_sem.at[which])
        copy.start()
        locals_.append(copy)
    greet(("row", "col", "dp"))

    def halves(size):
        return rows_at(me_d, size // 2)

    locals_[0].wait()
    tok_z = wire.spread("col", lambda p: tok.at[me_r, own], lambda p: tok.at[me_r, own])
    tok_r = [wire.spread("row", lambda p: tok.at[me_r, own], lambda p: tok.at[me_r, own])]
    locals_[1].wait()
    vec_r = wire.spread("row", lambda p: vecs.at[me_r], lambda p: vecs.at[me_r])
    locals_[2].wait()
    wq_half = halves(wq.shape[1])
    wq_r = wire.spread("row", lambda p: wq.at[me_r, wq_half], lambda p: wq.at[me_r, wq_half])
    locals_[3].wait()
    grad_z = wire.spread("col", lambda p: grad_cols.at[own], lambda p: grad_cols.at[own])
    locals_[4].wait()
    wo_half = halves(wo.shape[2])
    wo_z = wire.spread(
        "col", lambda p: wo.at[me_c, me_r, wo_half], lambda p: wo.at[me_c, me_r, wo_half]
    )

    for group in range(heads):
        width = 3 * HD
        bias_col[group * width : (group + 1) * width] = column_of(
            bias_q[:, group * width : (group + 1) * width]
        )
    seg = seg_row[...].astype(wide)
    for turn in range(cols):
        here = slice(turn * block, (turn + 1) * block)
        seg_col = column_of(seg[:, here])
        up = lax.broadcasted_iota(jnp.int32, (block, count), 0) + turn * block
        across = lax.broadcasted_iota(jnp.int32, (block, count), 1)
        allowed = (across <= up) & (seg == seg_col)
        mask[here] = jnp.where(allowed, 0.0, -jnp.inf)

    for step in range(1, cols):
        tok_z[step - 1].wait_recv()
        there = rows_at(lax.rem(me_c + cols - step, cols), block)
        tok_r.append(
            wire.spread(
                "row",
                lambda p, there=there: tok.at[me_r, there],
                lambda p, there=there: tok.at[me_r, there],
            )
        )
    wq_s = []
    for step in range(1, rows):
        wq_r[step - 1].wait_recv()
        peer = lax.rem(me_r + rows - step, rows)
        wq_s.append(wire.push(wq.at[peer, wq_half], wq.at[peer, wq_half], "dp", 1 - me_d))
    arrived(wo_z)
    wo_r = wire.spread(
        "row", lambda p: wo.at[:, me_r, wo_half], lambda p: wo.at[:, me_r, wo_half]
    )
    arrived(grad_z)
    grad_r = wire.spread(
        "row", lambda p: grad_cols.at[rows_at(p, block)], lambda p: grad_part.at[me_r]
    )
    locals_[5].wait()
    wf_half = halves(feats)
    wf_r = wire.spread("row", lambda p: wf.at[me_r, wf_half], lambda p: wf.at[me_r, wf_half])
    locals_[6].wait()
    wp_half = halves(wp.shape[1])
    wp_r = wire.spread("row", lambda p: wp.at[me_r, wp_half], lambda p: wp.at[me_r, wp_half])
    grad_part[me_r] = grad_cols[part]
    for copies in tok_r:
        arrived(copies)
    arrived(vec_r)
    arrived(wq_s)

    def norm_block(turn, carry):
        here = rows_at(turn, block)
        values = [tok[slot, here, :].astype(wide) for slot in range(rows)]
        mean = sum(jnp.sum(v, axis=1, keepdims=True) for v in values) / whole
        square = sum(jnp.sum(v * v, axis=1, keepdims=True) for v in values) / whole
        inv = lax.rsqrt(square - mean * mean + eps_norm)
        mean_one[here] = mean
        inv_one[here] = inv
        total_ = bias_col[...]
        for slot in range(rows):
            unit = (values[slot] - mean) * inv
            act = (unit * vecs[slot, 0:1, :] + vecs[slot, 1:2, :]).astype(low)
            act_one[slot, here, :] = act
            total_ = total_ + contract(wq[slot], act, 1, 1)
        qkv[:, here] = total_.astype(low)
        return carry

    lax.fori_loop(0, cols, norm_block, 0)

    def forward_head(head, carry):
        base = head * 3 * HD
        key = qkv[pl.ds(pl.multiple_of(base + HD, HD), HD), :]
        value = qkv[pl.ds(pl.multiple_of(base + 2 * HD, HD), HD), :]
        spot = rows_at(head, HD)
        for turn in range(cols):
            here = slice(turn * block, (turn + 1) * block)
            reach = (turn + 1) * block
            query = qkv[pl.ds(pl.multiple_of(base, HD), HD), here]
            scores = contract(query, key[:, :reach], 0, 0) * score_scale + mask[here, :reach]
            row_max = jnp.max(scores, axis=1, keepdims=True)
            raised = jnp.exp(scores - row_max)
            prob = raised * (1.0 / jnp.sum(raised, axis=1, keepdims=True))
            probs[head, here, :reach] = prob
            attn[spot, here] = contract(value[:, :reach], prob.astype(low), 1, 1).astype(low)
        return carry

    lax.fori_loop(0, heads, forward_head, 0)
    attn_z = wire.spread(
        "col", lambda p: attn.at[:, part], lambda p: attn_part.at[me_c]
    )
    attn_part[me_c] = attn[:, part]
    arrived(wo_r)
    wo_s = []
    for step in range(1, rows):
        peer = lax.rem(me_r + rows - step, rows)
        wo_s.append(wire.push(wo.at[:, peer, wo_half], wo.at[:, peer, wo_half], "dp", 1 - me_d))
    for step in range(1, cols):
        peer = lax.rem(me_c + cols - step, cols)
        wo_s.append(
            wire.push(wo.at[peer, me_r, wo_half], wo.at[peer, me_r, wo_half], "dp", 1 - me_d)
        )
    wf_s, wp_s = [], []
    for step in range(1, rows):
        peer = lax.rem(me_r + rows - step, rows)
        wf_r[step - 1].wait_recv()
        wf_s.append(wire.push(wf.at[peer, wf_half], wf.at[peer, wf_half], "dp", 1 - me_d))
    for step in range(1, rows):
        peer = lax.rem(me_r + rows - step, rows)
        wp_r[step - 1].wait_recv()
        wp_s.append(wire.push(wp.at[peer, wp_half], wp.at[peer, wp_half], "dp", 1 - me_d))
    arrived(wo_s)
    arrived(grad_r)
    arrived(attn_z)

    turned = [attn_part[slot].T for slot in range(cols)]
    mids = []
    for slot in range(rows):
        value = tok[slot, part, :].astype(wide) + vecs[slot, 4:5, :]
        for across in range(cols):
            value = value + contract(turned[across], wo[across, slot], 1, 0)
        mid[slot] = value
        mids.append(value)
    mean = sum(jnp.sum(v, axis=1, keepdims=True) for v in mids) / whole
    square = sum(jnp.sum(v * v, axis=1, keepdims=True) for v in mids) / whole
    inv = lax.rsqrt(square - mean * mean + eps_norm)
    inv_two[...] = inv
    for slot in range(rows):
        unit = (mids[slot] - mean) * inv
        unit_two[slot] = unit
        act_two[slot] = (unit * vecs[slot, 2:3, :] + vecs[slot, 3:4, :]).astype(low)
    act_cols[part] = act_two[me_r]
    arrived(wf_s)
    arrived(wp_s)
    pre = bias_f[...]
    grad_hidden = None
    for slot in range(rows):
        pre = pre + contract(act_two[slot], wf[slot], 1, 0)
        term = contract(grad_part[slot], wp[slot], 1, 1)
        grad_hidden = term if grad_hidden is None else grad_hidden + term
    curve = math.sqrt(2.0 / math.pi)
    square = pre * pre
    bend = jnp.tanh(curve * (pre + 0.044715 * (square * pre)))
    hid[part] = (0.5 * pre * (1.0 + bend)).astype(low)
    slope = 0.5 * (1.0 + bend) + 0.5 * pre * (1.0 - bend * bend) * (
        curve * (1.0 + 3.0 * 0.044715 * square)
    )
    grad_pre = (slope * grad_hidden).astype(low)
    gpre[part] = grad_pre
    for slot in range(rows):
        two_out[slot] = contract(grad_pre, wf[slot], 1, 1).astype(low)
    two_z = wire.spread(
        "col", lambda p: two_out.at[:, rows_at(p, piece)], lambda p: two_in.at[me_c]
    )
    hid_r = wire.spread("row", lambda p: hid.at[part], lambda p: hid.at[part])
    gpre_r = wire.spread("row", lambda p: gpre.at[part], lambda p: gpre.at[part])
    act_r = wire.spread("row", lambda p: act_two.at[p], lambda p: act_cols.at[part])
    two_in[me_c] = two_out[:, bit, :]
    arrived(two_z)

    two_sums, scaled, units = [], [], []
    for slot in range(rows):
        value = two_in[0, slot].astype(wide)
        for across in range(1, cols):
            value = value + two_in[across, slot].astype(wide)
        unit = unit_two[slot, bit, :]
        two_sums.append(value)
        units.append(unit)
        scaled.append(value * vecs[slot, 2:3, :])
        wide_out[slot] = jnp.concatenate(
            [
                jnp.sum(value * unit, axis=0, keepdims=True),
                jnp.sum(value, axis=0, keepdims=True),
            ],
            axis=0,
        )
    first_mean = sum(jnp.sum(v, axis=1, keepdims=True) for v in scaled) / whole
    second_mean = (
        sum(jnp.sum(v * u, axis=1, keepdims=True) for v, u in zip(scaled, units)) / whole
    )
    inv_piece = inv_two[bit, :]
    for slot in range(rows):
        value = grad_part[slot, bit, :].astype(wide) + inv_piece * (
            scaled[slot] - first_mean - units[slot] * second_mean
        )
        gm_piece[slot] = value.astype(low)
    mid_z = wire.spread("col", lambda p: gm_piece, lambda p: mid_part.at[:, bit])
    mid_part[:, bit, :] = gm_piece[...]
    arrived(mid_z)

    value = contract(wo[me_c, 0], mid_part[0], 1, 1)
    for slot in range(1, rows):
        value = value + contract(wo[me_c, slot], mid_part[slot], 1, 1)
    gattn[:, part] = value.astype(low)
    gattn_r = wire.spread("row", lambda p: gattn.at[:, part], lambda p: gattn.at[:, part])
    mid_r = wire.spread("row", lambda p: mid_part.at[p], lambda p: mid_cols.at[part])
    resid_r = wire.spread("row", lambda p: mid.at[p], lambda p: resid_own.at[part])
    mid_cols[part] = mid_part[me_r]
    resid_own[part] = mid[me_r]

    arrived(hid_r)
    arrived(gpre_r)
    arrived(act_r)
    sum_f[me_d] = contract(act_cols[...], gpre[...], 0, 0).astype(low)
    pair = [wire.push(sum_f.at[me_d], sum_f.at[me_d], "dp", 1 - me_d)]
    sum_p[me_d] = contract(hid[...], grad_cols[...], 0, 0).astype(low)
    pair.append(wire.push(sum_p.at[me_d], sum_p.at[me_d], "dp", 1 - me_d))
    ones = jnp.ones((8, count), low)
    sum_bf[me_d] = contract(ones, gpre[...], 1, 0)
    pair.append(wire.push(sum_bf.at[me_d], sum_bf.at[me_d], "dp", 1 - me_d))
    outward[...] = contract(hid[...], wp[me_r], 1, 0).astype(low)
    arrived(gattn_r)

    def backward_head(head, carry):
        base = head * 3 * HD
        spot_q = pl.ds(pl.multiple_of(base, HD), HD)
        spot_k = pl.ds(pl.multiple_of(base + HD, HD), HD)
        spot_v = pl.ds(pl.multiple_of(base + 2 * HD, HD), HD)
        spot = rows_at(head, HD)
        key, value = qkv[spot_k, :], qkv[spot_v, :]
        for turn in reversed(range(cols)):
            here = slice(turn * block, (turn + 1) * block)
            reach = (turn + 1) * block
            query = qkv[spot_q, here]
            grads = gattn[spot, here]
            dots = grads.astype(wide) * attn[spot, here].astype(wide)
            row_dot = jnp.sum(dots.T, axis=1, keepdims=True)
            prob = probs[head, here, :reach]
            grad_probs = contract(grads, value[:, :reach], 0, 0)
            grad_scores = (score_scale * prob * (grad_probs - row_dot)).astype(low)
            gqkv[spot_q, here] = contract(key[:, :reach], grad_scores, 1, 1).astype(low)
            term_k = contract(query, grad_scores, 1, 0)
            term_v = contract(grads, prob.astype(low), 1, 0)
            if turn == cols - 1:
                acc_k[...] = term_k
                acc_v[...] = term_v
            else:
                acc_k[:, :reach] += term_k
                acc_v[:, :reach] += term_v
        gqkv[spot_k, :] = acc_k[...].astype(low)
        gqkv[spot_v, :] = acc_v[...].astype(low)
        return carry

    lax.fori_loop(0, heads, backward_head, 0)
    sum_q[me_d] = contract(act_one[me_r], gqkv[...], 0, 1).astype(low)
    pair.append(wire.push(sum_q.at[me_d], sum_q.at[me_d], "dp", 1 - me_d))
    sum_bq[me_d] = contract(ones, gqkv[...], 1, 1)
    pair.append(wire.push(sum_bq.at[me_d], sum_bq.at[me_d], "dp", 1 - me_d))
    arrived(mid_r)
    sum_o[me_d] = contract(attn[...], mid_cols[...], 1, 0).astype(low)
    pair.append(wire.push(sum_o.at[me_d], sum_o.at[me_d], "dp", 1 - me_d))
    inward[...] = contract(gqkv[...], wq[me_r], 0, 0).astype(low)
    mid_own[...] = mid_cols[own]
    inv = inv_one[own]
    inv_own[...] = inv
    unit_own[...] = (tok[me_r, own].astype(wide) - mean_one[own]) * inv
    arrived(resid_r)
    arrived(pair)
    wire.drain()


def front(tokens, out_grad, segment_ids, w_qkv, w_out, w_fc, w_proj, bias_qkv, bias_fc, row_vectors):
    low, wide = jnp.bfloat16, jnp.float32
    rows, cols = lax.axis_size("row"), lax.axis_size("col")
    block, feats = tokens.shape
    count = block * cols
    piece = block // cols
    width, hidden = w_qkv.shape[1], w_fc.shape[1]
    heads = width // (3 * HD)
    shape = jax.ShapeDtypeStruct
    outs = [
        shape((2, feats, width), low),
        shape((2, w_out.shape[0], feats), low),
        shape((2, feats, hidden), low),
        shape((2, hidden, feats), low),
        shape((2, 8, width), wide),
        shape((2, 8, hidden), wide),
        shape((count, feats), low),
        shape((count, feats), low),
        shape((block, feats), wide),
        shape((block, 1), wide),
        shape((block, feats), low),
        shape((count, feats), wide),
        shape((rows, 2, feats), wide),
    ]
    buffers = [
        ((rows, count, feats), low),
        ((count, feats), low),
        ((rows, block, feats), low),
        ((rows, row_vectors.shape[0], feats), wide),
        ((rows, width, feats), low),
        ((cols, rows, w_out.shape[0], feats), low),
        ((rows, feats, hidden), low),
        ((rows, hidden, feats), low),
        ((rows, count, feats), low),
        ((width, count), low),
        ((width, 1), wide),
        ((count, count), wide),
        ((heads, count, count), wide),
        ((heads * HD, count), low),
        ((cols, heads * HD, block), low),
        ((rows, block, feats), wide),
        ((block, 1), wide),
        ((rows, block, feats), low),
        ((count, feats), low),
        ((rows, block, feats), wide),
        ((count, hidden), low),
        ((count, hidden), low),
        ((rows, block, feats), low),
        ((cols, rows, piece, feats), low),
        ((rows, piece, feats), low),
        ((rows, block, feats), low),
        ((count, feats), low),
        ((heads * HD, count), low),
        ((width, count), low),
        ((HD, count), wide),
        ((HD, count), wide),
        ((count, 1), wide),
        ((count, 1), wide),
    ]
    loose = pl.BlockSpec(memory_space=pl.ANY)
    near = pl.BlockSpec(memory_space=pltpu.VMEM)
    return pl.pallas_call(
        front_kernel,
        out_shape=outs,
        in_specs=[loose, loose, near, loose, loose, loose, loose, near, near, loose],
        out_specs=[near] * len(outs),
        scratch_shapes=[pltpu.VMEM(size, kind) for size, kind in buffers]
        + [
            pltpu.SemaphoreType.DMA((front_wires,)),
            pltpu.SemaphoreType.DMA((front_wires,)),
            pltpu.SemaphoreType.DMA((7,)),
        ],
        compiler_params=pltpu.CompilerParams(collective_id=20, has_side_effects=True),
    )(
        tokens,
        out_grad,
        segment_ids,
        w_qkv.T,
        w_out,
        w_fc,
        w_proj,
        bias_qkv[None],
        bias_fc[None],
        row_vectors,
    )


def local(
    tokens,
    out_grad,
    segment_ids,
    w_qkv,
    w_out,
    w_fc,
    w_proj,
    bias_qkv,
    bias_fc,
    row_vectors,
    mom_qkv,
    mom_out,
    mom_fc,
    mom_proj,
    mom_bias_qkv,
    mom_bias_fc,
    mom_rows,
):
    low = jnp.bfloat16
    score_scale = 1.0 / math.sqrt(HD)
    row_parts = lax.axis_size("row")
    col_parts = lax.axis_size("col")
    dp_parts = lax.axis_size("dp")
    own_tokens, own_features = tokens.shape
    token_count = own_tokens * col_parts
    feature_count = own_features * row_parts
    token_base = lax.axis_index("col") * own_tokens
    feature_base = lax.axis_index("row") * own_features

    def own_columns(whole):
        return lax.dynamic_slice_in_dim(whole, feature_base, own_features, 1)

    def own_block(whole):
        return lax.dynamic_slice(whole, (token_base, feature_base), (own_tokens, own_features))

    def own_rows(whole):
        return lax.dynamic_slice_in_dim(whole, token_base, own_tokens, 0)

    proj_flip = w_proj.T
    tokens_tall, grad_tall, out_tall = exchange(
        "col", [tokens, out_grad, w_out.T], [False] * 3, 0
    )
    grad_cols = grad_tall.reshape(token_count, own_features)
    matrices = [w_qkv, side_by_side(out_tall), w_fc, proj_flip]
    halved = dp_parts == 2
    pieces = matrices
    if halved:
        piece_size = own_features // 2
        pieces = [
            lax.dynamic_slice_in_dim(whole, lax.axis_index("dp") * piece_size, piece_size, 0)
            for whole in matrices
        ]
    token_slots, grad_slots, vector_slots, *gathered = exchange(
        "row",
        [
            tokens_tall.reshape(token_count, own_features),
            grad_cols.reshape(row_parts, -1, own_features),
            row_vectors,
        ]
        + pieces,
        [False, True, False] + [False] * 4,
        1,
    )
    if halved:
        gathered = [
            both.transpose(1, 0, 2, 3)
            for both in exchange("dp", gathered, [False] * 4, 19)
        ]
    qkv_cols, out_flip, fc_cols, proj_cols = [
        slots.reshape(feature_count, -1) for slots in gathered
    ]
    tokens_all = side_by_side(token_slots)
    grad_part = side_by_side(grad_slots)
    vectors_all = side_by_side(vector_slots)
    gain_one, shift_one, gain_two, shift_two, bias_out, _ = [
        vectors_all[which] for which in range(6)
    ]

    resid_in = tokens_all.astype(jnp.float32)
    mean_one, inv_one = norm_stats(resid_in)
    unit_one = (resid_in - mean_one) * inv_one
    act_one = (unit_one * gain_one + shift_one).astype(low)
    qkv_local = (product(act_one, qkv_cols, False) + bias_qkv).astype(low)
    heads_local = qkv_local.shape[1] // (3 * HD)
    qkv_tiles = qkv_local.reshape(token_count, heads_local, 3, HD).transpose(2, 1, 0, 3)
    query, key, value = qkv_tiles[0], qkv_tiles[1], qkv_tiles[2]
    segment_row = segment_ids[0]
    positions = jnp.arange(token_count, dtype=jnp.int32)
    allowed = (positions[None, :] <= positions[:, None]) & (
        segment_row[None, :] == segment_row[:, None]
    )
    scores = (
        jnp.einsum("hqe,hke->hqk", query, key, preferred_element_type=jnp.float32) * score_scale
    )
    scores = jnp.where(allowed[None], scores, -jnp.inf)
    row_max = jnp.max(scores, axis=2, keepdims=True)
    raised = jnp.exp(scores - row_max)
    probs = raised / jnp.sum(raised, axis=2, keepdims=True)
    prob_low = probs.astype(low)
    attended = jnp.einsum(
        "hqk,hke->hqe", prob_low, value, preferred_element_type=jnp.float32
    ).astype(low)
    attn_local = attended.transpose(1, 0, 2).reshape(token_count, heads_local * HD)
    part_tokens = token_count // row_parts
    part_base = lax.axis_index("row") * part_tokens

    def part_rows(whole):
        return lax.dynamic_slice_in_dim(whole, part_base, part_tokens, 0)

    (attn_slots,) = exchange("col", [part_rows(attn_local)], [False], 2)
    attn_part = jnp.concatenate([attn_slots[part] for part in range(col_parts)], axis=1)
    resid_mid = part_rows(resid_in) + product(attn_part, out_flip, True) + bias_out
    mean_two, inv_two = norm_stats(resid_mid)
    unit_two = (resid_mid - mean_two) * inv_two
    act_two = (unit_two * gain_two + shift_two).astype(low)
    hidden_pre = product(act_two, fc_cols, False) + bias_fc
    hidden = gelu_value(hidden_pre).astype(low)
    grad_hidden = product(grad_part, proj_cols, False)
    grad_pre = (gelu_slope(hidden_pre) * grad_hidden).astype(low)

    piece_tokens = part_tokens // col_parts
    piece_base = lax.axis_index("col") * piece_tokens

    def piece_rows(part):
        return lax.dynamic_slice_in_dim(part, piece_base, piece_tokens, 0)

    (two_slots,) = exchange(
        "col",
        [product(grad_pre, fc_cols, True).astype(low).reshape(col_parts, piece_tokens, -1)],
        [True],
        3,
    )
    grad_norm_two = total(two_slots)
    unit_two_piece = piece_rows(unit_two)
    scaled = grad_norm_two * gain_two
    first_mean = jnp.mean(scaled, axis=1, keepdims=True)
    second_mean = jnp.mean(scaled * unit_two_piece, axis=1, keepdims=True)
    grad_mid_piece = piece_rows(grad_part).astype(jnp.float32) + piece_rows(inv_two) * (
        scaled - first_mean - unit_two_piece * second_mean
    )
    grad_mid_low = grad_mid_piece.astype(low)
    (mid_slots,) = exchange("col", [grad_mid_low], [False], 4)
    mid_part = mid_slots.reshape(part_tokens, feature_count)
    out_rows = lax.dynamic_slice_in_dim(
        out_flip, lax.axis_index("col") * w_out.shape[0], w_out.shape[0], 1
    )
    grad_attn_part = product(mid_part, out_rows, False).astype(low)
    split = lambda rows: rows.reshape(part_tokens, row_parts, own_features).transpose(1, 0, 2)
    attn_grad_slots, mid_cols, act_two_cols, hidden_slots, grad_pre_slots, resid_cols = exchange(
        "row",
        [
            grad_attn_part,
            split(mid_part),
            split(act_two),
            hidden,
            grad_pre,
            split(resid_mid),
        ],
        [False, True, True, False, False, True],
        5,
    )
    grad_attn = (
        attn_grad_slots.reshape(token_count, heads_local, HD).transpose(1, 0, 2)
    )
    mid_cols = mid_cols.reshape(token_count, own_features)
    act_two_cols = act_two_cols.reshape(token_count, own_features)
    resid_cols = resid_cols.reshape(token_count, own_features)
    hidden_all = hidden_slots.reshape(token_count, -1)
    grad_pre_all = grad_pre_slots.reshape(token_count, -1)

    grad_value = jnp.einsum(
        "hqk,hqe->hke", prob_low, grad_attn, preferred_element_type=jnp.float32
    )
    grad_probs = jnp.einsum("hqe,hke->hqk", grad_attn, value, preferred_element_type=jnp.float32)
    row_dot = jnp.sum(
        grad_attn.astype(jnp.float32) * attended.astype(jnp.float32), axis=2, keepdims=True
    )
    grad_scores = (score_scale * probs * (grad_probs - row_dot)).astype(low)
    grad_query = jnp.einsum("hqk,hke->hqe", grad_scores, key, preferred_element_type=jnp.float32)
    grad_key = jnp.einsum("hqk,hqe->hke", grad_scores, query, preferred_element_type=jnp.float32)
    grad_qkv_low = (
        jnp.stack([grad_query.astype(low), grad_key.astype(low), grad_value.astype(low)], axis=0)
        .transpose(2, 1, 0, 3)
        .reshape(token_count, heads_local * 3 * HD)
    )

    grad_blocks = (
        inner_rows(own_columns(act_one), grad_qkv_low),
        inner_rows(attn_local, mid_cols),
        inner_rows(act_two_cols, grad_pre_all),
        inner_rows(hidden_all, grad_cols),
    )
    bias_blocks = jnp.concatenate(
        [
            jnp.sum(grad_qkv_low, axis=0, dtype=jnp.float32),
            jnp.sum(grad_pre_all, axis=0, dtype=jnp.float32),
        ]
    )[None]
    if dp_parts == 2:
        group_slots = exchange(
            "dp", [block.astype(low) for block in grad_blocks] + [bias_blocks], [False] * 5, 6
        )
        summed = [total(slots) for slots in group_slots]
    else:
        summed = [lax.psum(block.astype(low), "dp").astype(jnp.float32) for block in grad_blocks]
        summed.append(lax.psum(bias_blocks, "dp"))
    bias_sums = summed.pop()[0]
    summed = summed + [bias_sums[: bias_qkv.shape[0]], bias_sums[bias_qkv.shape[0] :]]

    weights = (w_qkv, w_out, w_fc, w_proj)
    moments = (mom_qkv, mom_out, mom_fc, mom_proj)
    flips = (False, True, False, True)
    new_moms = [beta_mom * moments[member] + summed[member] for member in range(4)]
    pushes = [
        (summed[member] + beta_mom * new_moms[member]).astype(low) for member in range(4)
    ]
    upright = [pushes[member].T if flips[member] else pushes[member] for member in range(4)]
    widest = max(piece.shape[1] for piece in upright)
    share = -(-widest // dp_parts)
    assert row_parts == len(upright)
    outgoing = jnp.stack(
        [
            jnp.pad(piece, ((0, 0), (0, share * dp_parts - piece.shape[1])))
            for piece in upright
        ]
    )
    outgoing = lax.dynamic_slice_in_dim(outgoing, lax.axis_index("dp") * share, share, 2)
    outward = product(hidden_all, proj_flip, True).astype(low)
    inward = product(grad_qkv_low, w_qkv, True).astype(low)
    arrived, block_slots, one_slots = exchange(
        ["row", "col", "col"],
        [
            outgoing,
            outward.reshape(col_parts, own_tokens, own_features),
            inward.reshape(col_parts, own_tokens, own_features),
        ],
        [True] * 3,
        7,
    )
    matrix = arrived.reshape(feature_count, share)
    gram_low = product(matrix, matrix, True).astype(low)
    edge = feature_count // 3
    spots = [(0, 0), (0, 1), (0, 2), (1, 1), (1, 2), (2, 2)]
    packed = jnp.concatenate(
        [
            gram_low[up * edge : (up + 1) * edge, across * edge : (across + 1) * edge]
            for up, across in spots
        ],
        axis=0,
    )
    block_out = (own_rows(resid_cols) + total(block_slots) + row_vectors[5]).astype(low)
    grad_norm_one = total(one_slots)
    unit_one_own = own_block(unit_one)
    scaled_one = grad_norm_one * row_vectors[0]
    stat_pair = jnp.stack(
        [jnp.sum(scaled_one, axis=1), jnp.sum(scaled_one * unit_one_own, axis=1)]
    )
    wide_terms = jnp.stack(
        [
            jnp.sum(grad_norm_two * unit_two_piece, axis=0),
            jnp.sum(grad_norm_two, axis=0),
        ]
    )
    wide_slot_terms = wide_terms.reshape(2, row_parts, own_features).transpose(1, 0, 2)
    if dp_parts == 2:
        stat_slots, wide_slots, half_slots = exchange(
            ["row", "row", "dp"],
            [stat_pair, wide_slot_terms, packed.reshape(dp_parts, -1, edge)],
            [False, True, True],
            8,
        )
        gram_half = total(half_slots).astype(low)
    else:
        stat_slots, wide_slots = exchange(
            "row", [stat_pair, wide_slot_terms], [False, True], 8
        )
        gram_half = lax.psum(packed, "dp")
    stat_sum = total(stat_slots)
    first_sum, second_sum = stat_sum[0][:, None], stat_sum[1][:, None]
    wide_sum = total(wide_slots)
    input_grad = own_rows(mid_cols).astype(jnp.float32) + own_rows(inv_one) * (
        scaled_one - first_sum / feature_count - unit_one_own * (second_sum / feature_count)
    )
    row_terms = jnp.stack(
        [
            jnp.sum(grad_norm_one * unit_one_own, axis=0),
            jnp.sum(grad_norm_one, axis=0),
            wide_sum[0],
            wide_sum[1],
            jnp.sum(own_rows(mid_cols), axis=0, dtype=jnp.float32),
            jnp.sum(out_grad, axis=0, dtype=jnp.float32),
        ]
    )
    quarter_slots, term_slots = exchange(
        "col",
        [gram_half.reshape(col_parts, -1, edge), row_terms],
        [True, False],
        9,
    )
    (whole_slots,) = exchange("col", [total(quarter_slots).astype(low)], [False], 10)
    gram_half = whole_slots.reshape(gram_half.shape)
    if dp_parts == 2:
        gram_slots, pair_slots = exchange(
            "dp", [gram_half, total(term_slots)], [False, False], 11
        )
        gram_half = gram_slots
    else:
        (pair_slots,) = exchange("dp", [total(term_slots)], [False], 11)
    grad_rows = total(pair_slots)
    tiles = gram_half.reshape(len(spots), edge, edge)
    found = {spot: tiles[which] for which, spot in enumerate(spots)}
    gram = jnp.concatenate(
        [
            jnp.concatenate(
                [
                    found[up, across] if across >= up else found[across, up].T
                    for across in range(3)
                ],
                axis=1,
            )
            for up in range(3)
        ],
        axis=0,
    ).astype(jnp.float32)
    factor, scale, gram_norm = polynomial_factor(gram)
    ortho = (scale * matrix.astype(jnp.float32) + matrix_product(factor, matrix)) * lax.rsqrt(
        gram_norm
    )
    (back,) = exchange(
        "row", [ortho.astype(low).reshape(row_parts, own_features, share)], [True], 12
    )
    if dp_parts == 2:
        (ortho_slots,) = exchange("dp", [back], [False], 13)
        orthos = jnp.concatenate([ortho_slots[part] for part in range(dp_parts)], axis=2)
    else:
        orthos = lax.all_gather(back, "dp", axis=2, tiled=True)
    new_weights = []
    for member in range(4):
        piece = orthos[member, :, : upright[member].shape[1]]
        if flips[member]:
            piece = piece.T
        longest = max(
            upright[member].shape[0] * row_parts, upright[member].shape[1] * col_parts
        )
        new_weights.append(
            weights[member].astype(jnp.float32)
            - rate_matrix * math.sqrt(longest) * piece.astype(jnp.float32)
        )

    vector_rate = rate_vector / math.sqrt(token_count * dp_parts)

    def vector_step(weight, gradient, moment):
        new_moment = beta_mom * moment + gradient
        return (weight - vector_rate * (gradient + beta_mom * new_moment), new_moment)

    new_bias_qkv, new_mom_bias_qkv = vector_step(bias_qkv, summed[4], mom_bias_qkv)
    new_bias_fc, new_mom_bias_fc = vector_step(bias_fc, summed[5], mom_bias_fc)
    new_rows, new_mom_rows = vector_step(row_vectors, grad_rows, mom_rows)
    return (
        block_out,
        input_grad,
        summed[0],
        summed[1],
        summed[2],
        summed[3],
        summed[4],
        summed[5],
        grad_rows,
        new_weights[0],
        new_weights[1],
        new_weights[2],
        new_weights[3],
        new_bias_qkv,
        new_bias_fc,
        new_rows,
        new_moms[0],
        new_moms[1],
        new_moms[2],
        new_moms[3],
        new_mom_bias_qkv,
        new_mom_bias_fc,
        new_mom_rows,
    )


def paired_local(
    tokens,
    out_grad,
    segment_ids,
    w_qkv,
    w_out,
    w_fc,
    w_proj,
    bias_qkv,
    bias_fc,
    row_vectors,
    mom_qkv,
    mom_out,
    mom_fc,
    mom_proj,
    mom_bias_qkv,
    mom_bias_fc,
    mom_rows,
):
    low = jnp.bfloat16
    score_scale = 1.0 / math.sqrt(HD)
    row_parts = lax.axis_size("row")
    col_parts = lax.axis_size("col")
    dp_parts = lax.axis_size("dp")
    own_tokens, own_features = tokens.shape
    token_count = own_tokens * col_parts
    feature_count = own_features * row_parts
    token_base = lax.axis_index("col") * own_tokens
    feature_base = lax.axis_index("row") * own_features

    def own_columns(whole):
        return lax.dynamic_slice_in_dim(whole, feature_base, own_features, 1)

    def own_block(whole):
        return lax.dynamic_slice(whole, (token_base, feature_base), (own_tokens, own_features))

    def own_rows(whole):
        return lax.dynamic_slice_in_dim(whole, token_base, own_tokens, 0)

    proj_flip = w_proj.T
    (
        slots_q, slots_o, slots_f, slots_p, slots_bq, slots_bf, outward, inward, unit_one_own,
        inv_own, mid_own, resid_all, wide_terms,
    ) = front(
        tokens, out_grad, segment_ids, w_qkv, w_out, w_fc, w_proj, bias_qkv, bias_fc, row_vectors
    )
    resid_own = own_rows(resid_all)
    summed = [total(slots) for slots in (slots_q, slots_o, slots_f, slots_p)]
    summed = summed + [total(slots_bq)[0], total(slots_bf)[0]]

    weights = (w_qkv, w_out, w_fc, w_proj)
    moments = (mom_qkv, mom_out, mom_fc, mom_proj)
    flips = (False, True, False, True)
    new_moms = [beta_mom * moments[member] + summed[member] for member in range(4)]
    pushes = [
        (summed[member] + beta_mom * new_moms[member]).astype(low) for member in range(4)
    ]
    upright = [pushes[member].T if flips[member] else pushes[member] for member in range(4)]
    widest = max(piece.shape[1] for piece in upright)
    share = -(-widest // dp_parts)
    assert row_parts == len(upright)
    outgoing = jnp.stack(
        [
            jnp.pad(piece, ((0, 0), (0, share * dp_parts - piece.shape[1])))
            for piece in upright
        ]
    )
    outgoing = lax.dynamic_slice_in_dim(outgoing, lax.axis_index("dp") * share, share, 2)
    arrived, block_slots, one_slots = exchange(
        ["row", "col", "col"],
        [
            outgoing,
            outward.reshape(col_parts, own_tokens, own_features),
            inward.reshape(col_parts, own_tokens, own_features),
        ],
        [True] * 3,
        7,
    )
    matrix = arrived.reshape(feature_count, share)
    gram_low = product(matrix, matrix, True).astype(low)
    edge = feature_count // 3
    spots = [(0, 0), (0, 1), (0, 2), (1, 1), (1, 2), (2, 2)]
    packed = jnp.concatenate(
        [
            gram_low[up * edge : (up + 1) * edge, across * edge : (across + 1) * edge]
            for up, across in spots
        ],
        axis=0,
    )
    block_out = (resid_own + total(block_slots) + row_vectors[5]).astype(low)
    grad_norm_one = total(one_slots)
    scaled_one = grad_norm_one * row_vectors[0]
    stat_pair = jnp.stack(
        [jnp.sum(scaled_one, axis=1), jnp.sum(scaled_one * unit_one_own, axis=1)]
    )
    wide_slot_terms = wide_terms
    if dp_parts == 2:
        stat_slots, wide_slots, half_slots = exchange(
            ["row", "row", "dp"],
            [stat_pair, wide_slot_terms, packed.reshape(dp_parts, -1, edge)],
            [False, True, True],
            8,
        )
        gram_half = total(half_slots).astype(low)
    else:
        stat_slots, wide_slots = exchange(
            "row", [stat_pair, wide_slot_terms], [False, True], 8
        )
        gram_half = lax.psum(packed, "dp")
    stat_sum = total(stat_slots)
    first_sum, second_sum = stat_sum[0][:, None], stat_sum[1][:, None]
    wide_sum = total(wide_slots)
    input_grad = mid_own.astype(jnp.float32) + inv_own * (
        scaled_one - first_sum / feature_count - unit_one_own * (second_sum / feature_count)
    )
    row_terms = jnp.stack(
        [
            jnp.sum(grad_norm_one * unit_one_own, axis=0),
            jnp.sum(grad_norm_one, axis=0),
            wide_sum[0],
            wide_sum[1],
            jnp.sum(mid_own, axis=0, dtype=jnp.float32),
            jnp.sum(out_grad, axis=0, dtype=jnp.float32),
        ]
    )
    quarter_slots, term_slots = exchange(
        "col",
        [gram_half.reshape(col_parts, -1, edge), row_terms],
        [True, False],
        9,
    )
    (whole_slots,) = exchange("col", [total(quarter_slots).astype(low)], [False], 10)
    gram_half = whole_slots.reshape(gram_half.shape)
    if dp_parts == 2:
        gram_slots, pair_slots = exchange(
            "dp", [gram_half, total(term_slots)], [False, False], 11
        )
        gram_half = gram_slots
    else:
        (pair_slots,) = exchange("dp", [total(term_slots)], [False], 11)
    grad_rows = total(pair_slots)
    tiles = gram_half.reshape(len(spots), edge, edge)
    found = {spot: tiles[which] for which, spot in enumerate(spots)}
    gram = jnp.concatenate(
        [
            jnp.concatenate(
                [
                    found[up, across] if across >= up else found[across, up].T
                    for across in range(3)
                ],
                axis=1,
            )
            for up in range(3)
        ],
        axis=0,
    ).astype(jnp.float32)
    factor, scale, gram_norm = polynomial_factor(gram)
    ortho = (scale * matrix.astype(jnp.float32) + matrix_product(factor, matrix)) * lax.rsqrt(
        gram_norm
    )
    (back,) = exchange(
        "row", [ortho.astype(low).reshape(row_parts, own_features, share)], [True], 12
    )
    if dp_parts == 2:
        (ortho_slots,) = exchange("dp", [back], [False], 13)
        orthos = jnp.concatenate([ortho_slots[part] for part in range(dp_parts)], axis=2)
    else:
        orthos = lax.all_gather(back, "dp", axis=2, tiled=True)
    new_weights = []
    for member in range(4):
        piece = orthos[member, :, : upright[member].shape[1]]
        if flips[member]:
            piece = piece.T
        longest = max(
            upright[member].shape[0] * row_parts, upright[member].shape[1] * col_parts
        )
        new_weights.append(
            weights[member].astype(jnp.float32)
            - rate_matrix * math.sqrt(longest) * piece.astype(jnp.float32)
        )

    vector_rate = rate_vector / math.sqrt(token_count * dp_parts)

    def vector_step(weight, gradient, moment):
        new_moment = beta_mom * moment + gradient
        return (weight - vector_rate * (gradient + beta_mom * new_moment), new_moment)

    new_bias_qkv, new_mom_bias_qkv = vector_step(bias_qkv, summed[4], mom_bias_qkv)
    new_bias_fc, new_mom_bias_fc = vector_step(bias_fc, summed[5], mom_bias_fc)
    new_rows, new_mom_rows = vector_step(row_vectors, grad_rows, mom_rows)
    return (
        block_out,
        input_grad,
        summed[0],
        summed[1],
        summed[2],
        summed[3],
        summed[4],
        summed[5],
        grad_rows,
        new_weights[0],
        new_weights[1],
        new_weights[2],
        new_weights[3],
        new_bias_qkv,
        new_bias_fc,
        new_rows,
        new_moms[0],
        new_moms[1],
        new_moms[2],
        new_moms[3],
        new_mom_bias_qkv,
        new_mom_bias_fc,
        new_mom_rows,
    )


def solution(mesh):
    placed = (
        P(("dp", "col"), "row"),
        P(("dp", "col"), "row"),
        P("dp", None),
        P("row", "col"),
        P("col", "row"),
        P("row", "col"),
        P("col", "row"),
        P("col"),
        P("col"),
        P(None, "row"),
        P("row", "col"),
        P("col", "row"),
        P("row", "col"),
        P("col", "row"),
        P("col"),
        P("col"),
        P(None, "row"),
    )
    return jax.shard_map(
        paired_local if mesh.shape["dp"] == 2 else local,
        mesh=mesh,
        in_specs=placed,
        out_specs=(
            P(("dp", "col"), "row"),
            P(("dp", "col"), "row"),
            P("row", "col"),
            P("col", "row"),
            P("row", "col"),
            P("col", "row"),
            P("col"),
            P("col"),
            P(None, "row"),
            P("row", "col"),
            P("col", "row"),
            P("row", "col"),
            P("col", "row"),
            P("col"),
            P("col"),
            P(None, "row"),
            P("row", "col"),
            P("col", "row"),
            P("row", "col"),
            P("col", "row"),
            P("col"),
            P("col"),
            P(None, "row"),
        ),
        check_vma=False,
    )
```

```python
import functools
import math

import jax
import jax.numpy as jnp
from jax import lax
from jax.experimental import pallas as pl
from jax.experimental.pallas import tpu as pltpu
from jax.sharding import PartitionSpec as P

HD = 64
NS_STEPS = 2


eps_norm = 1e-05
eps_gram = 1e-06
coef_a = 3.4445
coef_b = -4.775
coef_c = 2.0315
beta_mom = 0.95
rate_matrix = 0.03
rate_vector = 0.6


def gelu_value(values):
    return jax.nn.gelu(values, approximate=True)


def gelu_slope(values):
    return jax.vjp(gelu_value, values)[1](jnp.ones_like(values))[0]


def product(left_side, right_side, flip_right):
    if flip_right:
        return lax.dot_general(
            left_side, right_side, (((1,), (1,)), ((), ())), preferred_element_type=jnp.float32
        )
    return jnp.dot(left_side, right_side, preferred_element_type=jnp.float32)


def inner_rows(left_side, right_side):
    return lax.dot_general(
        left_side, right_side, (((0,), (0,)), ((), ())), preferred_element_type=jnp.float32
    )


def exchange_kernel(axes, parts, kinds, *refs):
    count = len(kinds)
    sources, targets = refs[:count], refs[count : 2 * count]
    send_sem, recv_sem, local_sem = refs[2 * count :]
    barrier = pltpu.get_barrier_semaphore()
    met = 0
    for axis in sorted(set(axes)):
        axis_parts = parts[axes.index(axis)]
        for step in range(1, axis_parts):
            peer = lax.rem(lax.axis_index(axis) + step, axis_parts)
            pl.semaphore_signal(
                barrier, inc=1, device_id={axis: peer}, device_id_type=pl.DeviceIdType.MESH
            )
            met += 1
    pl.semaphore_wait(barrier, met)
    copies = []
    for which in range(count):
        axis = axes[which]
        me = lax.axis_index(axis)
        for step in range(1, parts[which]):
            peer = lax.rem(me + step, parts[which])
            copy = pltpu.make_async_remote_copy(
                src_ref=sources[which].at[peer] if kinds[which] else sources[which],
                dst_ref=targets[which].at[me],
                send_sem=send_sem.at[which, step - 1],
                recv_sem=recv_sem.at[which, step - 1],
                device_id={axis: peer},
                device_id_type=pl.DeviceIdType.MESH,
            )
            copy.start()
            copies.append(copy)
    for which in range(count):
        me = lax.axis_index(axes[which])
        copy = pltpu.make_async_copy(
            sources[which].at[me] if kinds[which] else sources[which],
            targets[which].at[me],
            local_sem.at[which],
        )
        copy.start()
        copies.append(copy)
    for copy in copies:
        copy.wait()


def exchange(axes, arrays, kinds, name_id):
    count = len(arrays)
    if isinstance(axes, str):
        axes = [axes] * count
    parts = [lax.axis_size(axis) for axis in axes]
    shapes = [
        jax.ShapeDtypeStruct(array.shape if kind else (part,) + array.shape, array.dtype)
        for array, kind, part in zip(arrays, kinds, parts)
    ]
    return pl.pallas_call(
        functools.partial(exchange_kernel, tuple(axes), tuple(parts), tuple(kinds)),
        out_shape=shapes,
        in_specs=[pl.BlockSpec(memory_space=pltpu.VMEM)] * count,
        out_specs=[pl.BlockSpec(memory_space=pltpu.VMEM)] * count,
        scratch_shapes=[
            pltpu.SemaphoreType.DMA((count, max(parts) - 1)),
            pltpu.SemaphoreType.DMA((count, max(parts) - 1)),
            pltpu.SemaphoreType.DMA((count,)),
        ],
        compiler_params=pltpu.CompilerParams(collective_id=name_id, has_side_effects=True),
    )(*arrays)


def total(slots):
    return jnp.sum(slots.astype(jnp.float32), axis=0)


def side_by_side(slots):
    return jnp.concatenate([slots[part] for part in range(slots.shape[0])], axis=1)


def norm_stats(values):
    mean_row = jnp.mean(values, axis=1, keepdims=True)
    square = jnp.mean(values * values, axis=1, keepdims=True)
    inv_std = lax.rsqrt(square - mean_row * mean_row + eps_norm)
    return mean_row, inv_std


def matrix_product(left_side, right_side):
    return jnp.dot(
        left_side.astype(jnp.bfloat16),
        right_side.astype(jnp.bfloat16),
        preferred_element_type=jnp.float32,
    )


def polynomial_factor(gram_matrix):
    gram_norm = jnp.sqrt(jnp.sum(gram_matrix * gram_matrix)) + eps_gram
    gram_now = gram_matrix / gram_norm
    poly_before = None
    for repeat in range(NS_STEPS):
        poly = coef_b * gram_now + coef_c * matrix_product(gram_now, gram_now)
        if poly_before is None:
            factor = poly
            scale = coef_a
        else:
            factor = coef_a * factor + scale * poly + matrix_product(poly, factor)
            scale = scale * coef_a
        if repeat + 1 < NS_STEPS:
            half = coef_a * gram_now + matrix_product(poly, gram_now)
            gram_now = coef_a * half + matrix_product(half, poly)
        poly_before = poly
    return factor, scale, gram_norm


def contract(left_side, right_side, left_dim, right_dim):
    return lax.dot_general(
        left_side,
        right_side,
        (((left_dim,), (right_dim,)), ((), ())),
        preferred_element_type=jnp.float32,
    )


def column_of(row_values):
    size = row_values.shape[1]
    up = lax.broadcasted_iota(jnp.int32, (size, size), 0)
    across = lax.broadcasted_iota(jnp.int32, (size, size), 1)
    return jnp.sum(jnp.where(up == across, row_values, 0.0), axis=1, keepdims=True)


class Wire:
    def __init__(self, send_sem, recv_sem):
        self.send_sem, self.recv_sem = send_sem, recv_sem
        self.used = 0
        self.live = []

    def push(self, source, target, axis, peer):
        copy = pltpu.make_async_remote_copy(
            src_ref=source,
            dst_ref=target,
            send_sem=self.send_sem.at[self.used],
            recv_sem=self.recv_sem.at[self.used],
            device_id={axis: peer},
            device_id_type=pl.DeviceIdType.MESH,
        )
        self.used += 1
        copy.start()
        self.live.append(copy)
        return copy

    def spread(self, axis, source_of, target_of):
        parts = lax.axis_size(axis)
        me = lax.axis_index(axis)
        copies = []
        for step in range(1, parts):
            peer = lax.rem(me + step, parts)
            copies.append(self.push(source_of(peer), target_of(peer), axis, peer))
        return copies

    def drain(self):
        for copy in self.live:
            copy.wait_send()


def greet(axes):
    barrier = pltpu.get_barrier_semaphore()
    met = 0
    for axis in axes:
        parts = lax.axis_size(axis)
        for step in range(1, parts):
            peer = lax.rem(lax.axis_index(axis) + step, parts)
            pl.semaphore_signal(
                barrier, inc=1, device_id={axis: peer}, device_id_type=pl.DeviceIdType.MESH
            )
            met += 1
    return lambda: pl.semaphore_wait(barrier, met)


def arrived(copies):
    for copy in copies:
        copy.wait_recv()


def rows_at(index, size):
    return pl.ds(pl.multiple_of(index * size, size), size)


step_wires = 180


def step_kernel(*refs):
    low, wide = jnp.bfloat16, jnp.float32
    (
        tok_in, grad_in, seg_row, wq_in, wo_in, wf_in, wp_in, bias_q, bias_f, vec_in,
        mom_q_in, mom_o_in, mom_f_in, mom_p_in,
        sum_q, sum_o, sum_f, sum_p, sum_bq, sum_bf, block_out, input_grad, grad_rows, back,
        tok, grad_cols, grad_turn, grad_part, vecs, wq_own, wq, wo, wf, wp, act_one, qkv,
        bias_col, gains, mask, probs,
        attn, attn_part, unit_two, inv_two, act_two, act_cols, mid, resid, hid, gpre, two_out,
        two_in, gm_piece, mid_part, mid_cols, gattn, gqkv, acc_k, acc_v, mean_one, inv_one,
        wide_out, wide_in, outward, outward_in, inward, inward_in, stat_out, stat_in,
        term_out, term_in, term_pair, mom_q, mom_o, mom_f, mom_p, pushed, matrix, packed,
        packed_in, halved, quarter_in, gathered, gram, ortho,
        send_sem, recv_sem, local_sem,
    ) = refs
    rows, cols = lax.axis_size("row"), lax.axis_size("col")
    me_r, me_c, me_d = lax.axis_index("row"), lax.axis_index("col"), lax.axis_index("dp")
    other = 1 - me_d
    feats, count = tok.shape[1], tok.shape[2]
    whole = feats * rows
    block = count // cols
    piece = block // cols
    heads = qkv.shape[0] // (3 * HD)
    score_scale = 1.0 / math.sqrt(HD)
    own = rows_at(me_c, block)
    part = rows_at(me_r, block)
    bit = rows_at(me_c, piece)
    wire = Wire(send_sem, recv_sem)
    met = greet(("row", "col", "dp"))
    locals_ = []
    for which, (source, target) in enumerate(
        [
            (tok_in, tok.at[me_r, :, own]),
            (vec_in, vecs.at[me_r]),
            (wq_in, wq_own),
            (grad_in, grad_cols.at[:, own]),
            (wo_in, wo.at[me_c, me_r]),
            (wf_in, wf.at[me_r]),
            (wp_in, wp.at[me_r]),
            (mom_f_in, mom_f),
            (mom_p_in, mom_p),
            (mom_q_in, mom_q),
            (mom_o_in, mom_o),
        ]
    ):
        copy = pltpu.make_async_copy(source, target, local_sem.at[which])
        copy.start()
        locals_.append(copy)

    def halves(size):
        return rows_at(me_d, size // 2)

    locals_[2].wait()
    wq[me_r] = wq_own[...].T
    locals_[0].wait()
    met()
    tok_z = wire.spread("col", lambda p: tok.at[me_r, :, own], lambda p: tok.at[me_r, :, own])
    tok_r = [wire.spread("row", lambda p: tok.at[me_r, :, own], lambda p: tok.at[me_r, :, own])]
    locals_[1].wait()
    vec_r = wire.spread("row", lambda p: vecs.at[me_r], lambda p: vecs.at[me_r])
    wq_half = halves(wq.shape[1])
    wq_r = wire.spread("row", lambda p: wq.at[me_r, wq_half], lambda p: wq.at[me_r, wq_half])
    locals_[3].wait()
    grad_z = wire.spread("col", lambda p: grad_cols.at[:, own], lambda p: grad_cols.at[:, own])
    locals_[4].wait()
    wo_half = halves(wo.shape[2])
    wo_z = wire.spread(
        "col", lambda p: wo.at[me_c, me_r, wo_half], lambda p: wo.at[me_c, me_r, wo_half]
    )

    span = 3 * HD
    for group in range(heads):
        here = slice(group * span, (group + 1) * span)
        bias_col[here] = column_of(bias_q[:, here])
    seg = seg_row[...].astype(wide)
    for turn in range(cols):
        here = slice(turn * block, (turn + 1) * block)
        seg_col = column_of(seg[:, here])
        up = lax.broadcasted_iota(jnp.int32, (block, count), 0) + turn * block
        across = lax.broadcasted_iota(jnp.int32, (block, count), 1)
        allowed = (across <= up) & (seg == seg_col)
        mask[here] = jnp.where(allowed, 0.0, -jnp.inf)

    for step in range(1, cols):
        tok_z[step - 1].wait_recv()
        there = rows_at(lax.rem(me_c + cols - step, cols), block)
        tok_r.append(
            wire.spread(
                "row",
                lambda p, there=there: tok.at[me_r, :, there],
                lambda p, there=there: tok.at[me_r, :, there],
            )
        )
    wq_s = []
    for step in range(1, rows):
        wq_r[step - 1].wait_recv()
        peer = lax.rem(me_r + rows - step, rows)
        wq_s.append(wire.push(wq.at[peer, wq_half], wq.at[peer, wq_half], "dp", other))
    arrived(wo_z)
    wo_r = wire.spread(
        "row", lambda p: wo.at[:, me_r, wo_half], lambda p: wo.at[:, me_r, wo_half]
    )
    arrived(grad_z)
    grad_r = wire.spread(
        "row",
        lambda p: grad_cols.at[:, rows_at(p, block)],
        lambda p: grad_turn.at[me_r],
    )
    locals_[5].wait()
    wf_half = halves(feats)
    wf_r = wire.spread("row", lambda p: wf.at[me_r, wf_half], lambda p: wf.at[me_r, wf_half])
    locals_[6].wait()
    wp_r = wire.spread("row", lambda p: wp.at[me_r, wf_half], lambda p: wp.at[me_r, wf_half])
    grad_turn[me_r] = grad_cols[:, part]
    arrived(vec_r)
    for slot in range(rows):
        for which in range(2):
            gains[slot, which] = column_of(vecs[slot, which : which + 1, :])
    for copies in tok_r:
        arrived(copies)
    arrived(wq_s)

    def norm_block(turn, carry):
        here = rows_at(turn, block)
        values = [tok[slot, :, here].astype(wide) for slot in range(rows)]
        mean = sum(jnp.sum(v, axis=0, keepdims=True) for v in values) / whole
        square = sum(jnp.sum(v * v, axis=0, keepdims=True) for v in values) / whole
        inv = lax.rsqrt(square - mean * mean + eps_norm)
        mean_one[:, here] = mean
        inv_one[:, here] = inv
        total_ = bias_col[...]
        for slot in range(rows):
            unit = (values[slot] - mean) * inv
            act = (unit * gains[slot, 0] + gains[slot, 1]).astype(low)
            act_one[slot, :, here] = act
            total_ = total_ + contract(wq[slot], act, 1, 0)
        qkv[:, here] = total_.astype(low)
        return carry

    lax.fori_loop(0, cols, norm_block, 0)

    def forward_head(head, carry):
        base = head * span
        key = qkv[pl.ds(pl.multiple_of(base + HD, HD), HD), :]
        value = qkv[pl.ds(pl.multiple_of(base + 2 * HD, HD), HD), :]
        spot = rows_at(head, HD)
        for turn in range(cols):
            here = slice(turn * block, (turn + 1) * block)
            reach = (turn + 1) * block
            query = qkv[pl.ds(pl.multiple_of(base, HD), HD), here]
            scores = contract(query, key[:, :reach], 0, 0) * score_scale + mask[here, :reach]
            row_max = jnp.max(scores, axis=1, keepdims=True)
            raised = jnp.exp(scores - row_max)
            prob = raised * (1.0 / jnp.sum(raised, axis=1, keepdims=True))
            probs[head, here, :reach] = prob
            attn[spot, here] = contract(value[:, :reach], prob.astype(low), 1, 1).astype(low)
        return carry

    lax.fori_loop(0, heads, forward_head, 0)
    attn_z = wire.spread("col", lambda p: attn.at[:, part], lambda p: attn_part.at[me_c])
    attn_part[me_c] = attn[:, part]
    arrived(wo_r)
    wo_s = []
    for step in range(1, rows):
        peer = lax.rem(me_r + rows - step, rows)
        wo_s.append(wire.push(wo.at[:, peer, wo_half], wo.at[:, peer, wo_half], "dp", other))
    for step in range(1, cols):
        peer = lax.rem(me_c + cols - step, cols)
        wo_s.append(wire.push(wo.at[peer, me_r, wo_half], wo.at[peer, me_r, wo_half], "dp", other))
    wf_s, wp_s = [], []
    for step in range(1, rows):
        peer = lax.rem(me_r + rows - step, rows)
        wf_r[step - 1].wait_recv()
        wf_s.append(wire.push(wf.at[peer, wf_half], wf.at[peer, wf_half], "dp", other))
    for step in range(1, rows):
        peer = lax.rem(me_r + rows - step, rows)
        wp_r[step - 1].wait_recv()
        wp_s.append(wire.push(wp.at[peer, wf_half], wp.at[peer, wf_half], "dp", other))
    arrived(grad_r)
    for slot in range(rows):
        grad_part[slot] = grad_turn[slot].T
        mid[slot] = tok[slot, :, part].T.astype(wide) + vecs[slot, 4:5, :]
    arrived(wo_s)
    arrived(attn_z)

    turned = [attn_part[slot].T for slot in range(cols)]
    mids = []
    for slot in range(rows):
        value = mid[slot]
        for across in range(cols):
            value = value + contract(turned[across], wo[across, slot], 1, 0)
        mid[slot] = value
        mids.append(value)
    mean = sum(jnp.sum(v, axis=1, keepdims=True) for v in mids) / whole
    square = sum(jnp.sum(v * v, axis=1, keepdims=True) for v in mids) / whole
    inv = lax.rsqrt(square - mean * mean + eps_norm)
    inv_two[...] = inv
    for slot in range(rows):
        unit = (mids[slot] - mean) * inv
        unit_two[slot] = unit
        act_two[slot] = (unit * vecs[slot, 2:3, :] + vecs[slot, 3:4, :]).astype(low)
    act_cols[part] = act_two[me_r]
    arrived(wf_s)
    arrived(wp_s)
    pre = bias_f[...]
    grad_hidden = None
    for slot in range(rows):
        pre = pre + contract(act_two[slot], wf[slot], 1, 0)
        term = contract(grad_part[slot], wp[slot], 1, 0)
        grad_hidden = term if grad_hidden is None else grad_hidden + term
    curve = math.sqrt(2.0 / math.pi)
    square = pre * pre
    bend = jnp.tanh(curve * (pre + 0.044715 * (square * pre)))
    hid[part] = (0.5 * pre * (1.0 + bend)).astype(low)
    slope = 0.5 * (1.0 + bend) + 0.5 * pre * (1.0 - bend * bend) * (
        curve * (1.0 + 3.0 * 0.044715 * square)
    )
    grad_pre = (slope * grad_hidden).astype(low)
    gpre[part] = grad_pre
    for slot in range(rows):
        two_out[slot] = contract(grad_pre, wf[slot], 1, 1).astype(low)
    two_z = wire.spread(
        "col", lambda p: two_out.at[:, rows_at(p, piece)], lambda p: two_in.at[me_c]
    )
    hid_r = wire.spread("row", lambda p: hid.at[part], lambda p: hid.at[part])
    gpre_r = wire.spread("row", lambda p: gpre.at[part], lambda p: gpre.at[part])
    act_r = wire.spread("row", lambda p: act_two.at[p], lambda p: act_cols.at[part])
    two_in[me_c] = two_out[:, bit, :]
    arrived(two_z)

    scaled, units = [], []
    for slot in range(rows):
        value = two_in[0, slot].astype(wide)
        for across in range(1, cols):
            value = value + two_in[across, slot].astype(wide)
        unit = unit_two[slot, bit, :]
        units.append(unit)
        scaled.append(value * vecs[slot, 2:3, :])
        wide_out[slot, 0:1] = jnp.sum(value * unit, axis=0, keepdims=True)
        wide_out[slot, 1:2] = jnp.sum(value, axis=0, keepdims=True)
    first_mean = sum(jnp.sum(v, axis=1, keepdims=True) for v in scaled) / whole
    second_mean = (
        sum(jnp.sum(v * u, axis=1, keepdims=True) for v, u in zip(scaled, units)) / whole
    )
    inv_piece = inv_two[bit, :]
    for slot in range(rows):
        value = grad_part[slot, bit, :].astype(wide) + inv_piece * (
            scaled[slot] - first_mean - units[slot] * second_mean
        )
        gm_piece[slot] = value.astype(low)
    mid_z = wire.spread("col", lambda p: gm_piece, lambda p: mid_part.at[:, bit])
    mid_part[:, bit, :] = gm_piece[...]
    arrived(mid_z)

    value = contract(wo[me_c, 0], mid_part[0], 1, 1)
    for slot in range(1, rows):
        value = value + contract(wo[me_c, slot], mid_part[slot], 1, 1)
    gattn[:, part] = value.astype(low)
    gattn_r = wire.spread("row", lambda p: gattn.at[:, part], lambda p: gattn.at[:, part])
    mid_r = wire.spread("row", lambda p: mid_part.at[p], lambda p: mid_cols.at[part])
    mid_cols[part] = mid_part[me_r]
    wide_r = wire.spread("row", lambda p: wide_out.at[p], lambda p: wide_in.at[me_r])
    wide_in[me_r] = wide_out[me_r]
    giver = me_r == me_c
    resid_r = []
    base = wire.used
    wire.used += rows
    for step in range(1, rows):
        peer = lax.rem(me_r + step, rows)
        resid_r.append(
            pltpu.make_async_remote_copy(
                src_ref=mid.at[peer],
                dst_ref=resid,
                send_sem=send_sem.at[base + step],
                recv_sem=recv_sem.at[base],
                device_id={"row": peer},
                device_id_type=pl.DeviceIdType.MESH,
            )
        )

    @pl.when(giver)
    def _():
        for copy in resid_r:
            copy.start()
        resid[...] = mid[me_r]

    arrived(hid_r)
    arrived(gpre_r)
    arrived(act_r)
    sum_f[me_d] = contract(act_cols[...], gpre[...], 0, 0).astype(low)
    pair_f = wire.push(sum_f.at[me_d], sum_f.at[me_d], "dp", other)
    sum_p[me_d] = contract(grad_cols[...], hid[...], 1, 0).astype(low)
    pair_p = wire.push(sum_p.at[me_d], sum_p.at[me_d], "dp", other)
    ones = jnp.ones((8, count), low)
    sum_bf[me_d] = contract(ones, gpre[...], 1, 0)
    pair = [wire.push(sum_bf.at[me_d], sum_bf.at[me_d], "dp", other)]
    outward[...] = contract(wp[me_r], hid[...], 1, 1).astype(low)
    outward_z = wire.spread(
        "col", lambda p: outward.at[:, rows_at(p, block)], lambda p: outward_in.at[me_c]
    )
    outward_in[me_c] = outward[:, own]

    def push_of(sums, moment):
        gradient = sums[0].astype(wide) + sums[1].astype(wide)
        return (gradient + beta_mom * (beta_mom * moment[...] + gradient)).astype(low)

    share = matrix.shape[1]
    mine = rows_at(me_d, share)
    push_r = []
    base = wire.used
    wire.used += rows
    for step in range(1, rows):
        peer = lax.rem(me_r + step, rows)
        push_r.append(
            pltpu.make_async_remote_copy(
                src_ref=pushed.at[peer, :, mine],
                dst_ref=matrix.at[rows_at(me_r, feats)],
                send_sem=send_sem.at[base + step],
                recv_sem=recv_sem.at[base + step],
                device_id={"row": peer},
                device_id_type=pl.DeviceIdType.MESH,
            )
        )

    def launch(first, last):
        for step in range(1, rows):
            peer = lax.rem(me_r + step, rows)

            @pl.when((peer >= first) & (peer < last))
            def _(copy=push_r[step - 1]):
                copy.start()

    pushed[0] = jnp.zeros(pushed.shape[1:], low)
    pushed[1] = jnp.zeros(pushed.shape[1:], low)
    for which in range(7, 11):
        locals_[which].wait()
    pair_f.wait_recv()
    pair_p.wait_recv()
    pushed[2] = push_of(sum_f, mom_f)
    pushed[3] = push_of(sum_p, mom_p)
    launch(2, rows)
    arrived(gattn_r)

    def backward_head(head, carry):
        base = head * span
        spot_q = pl.ds(pl.multiple_of(base, HD), HD)
        spot_k = pl.ds(pl.multiple_of(base + HD, HD), HD)
        spot_v = pl.ds(pl.multiple_of(base + 2 * HD, HD), HD)
        spot = rows_at(head, HD)
        key, value = qkv[spot_k, :], qkv[spot_v, :]
        for turn in reversed(range(cols)):
            here = slice(turn * block, (turn + 1) * block)
            reach = (turn + 1) * block
            query = qkv[spot_q, here]
            grads = gattn[spot, here]
            dots = grads.astype(wide) * attn[spot, here].astype(wide)
            row_dot = jnp.sum(dots.T, axis=1, keepdims=True)
            prob = probs[head, here, :reach]
            grad_probs = contract(grads, value[:, :reach], 0, 0)
            grad_scores = (score_scale * prob * (grad_probs - row_dot)).astype(low)
            gqkv[spot_q, here] = contract(key[:, :reach], grad_scores, 1, 1).astype(low)
            term_k = contract(query, grad_scores, 1, 0)
            term_v = contract(grads, prob.astype(low), 1, 0)
            if turn == cols - 1:
                acc_k[...] = term_k
                acc_v[...] = term_v
            else:
                acc_k[:, :reach] += term_k
                acc_v[:, :reach] += term_v
        gqkv[spot_k, :] = acc_k[...].astype(low)
        gqkv[spot_v, :] = acc_v[...].astype(low)
        return carry

    lax.fori_loop(0, heads, backward_head, 0)
    sum_q[me_d] = contract(act_one[me_r], gqkv[...], 1, 1).astype(low)
    pair_q = wire.push(sum_q.at[me_d], sum_q.at[me_d], "dp", other)
    arrived(mid_r)
    sum_o[me_d] = contract(attn[...], mid_cols[...], 1, 0).astype(low)
    pair_o = wire.push(sum_o.at[me_d], sum_o.at[me_d], "dp", other)
    sum_bq[me_d] = contract(ones, gqkv[...], 1, 1)
    pair.append(wire.push(sum_bq.at[me_d], sum_bq.at[me_d], "dp", other))
    inward[...] = contract(wq_own[...], gqkv[...], 1, 0).astype(low)
    inward_z = wire.spread(
        "col", lambda p: inward.at[:, rows_at(p, block)], lambda p: inward_in.at[me_c]
    )
    inward_in[me_c] = inward[:, own]
    pair_q.wait_recv()
    pushed[0, :, : mom_q.shape[1]] = push_of(sum_q, mom_q)
    pair_o.wait_recv()
    pushed[1, :, : mom_o.shape[0]] = push_of(sum_o, mom_o).T
    launch(0, 2)
    matrix[rows_at(me_r, feats)] = pushed[me_r, :, mine]

    arrived(outward_z)

    @pl.when(jnp.logical_not(giver))
    def _():
        resid_r[0].wait_recv()

    def slots_of(slots):
        value = slots[0].astype(wide)
        for across in range(1, slots.shape[0]):
            value = value + slots[across].astype(wide)
        return value

    block_out[...] = (
        resid[...].T + slots_of(outward_in) + column_of(vecs[me_r, 5:6, :])
    ).astype(low)
    arrived(inward_z)
    grad_one = slots_of(inward_in)
    inv = inv_one[:, own]
    unit = (tok[me_r, :, own].astype(wide) - mean_one[:, own]) * inv
    scaled_one = grad_one * gains[me_r, 0]
    stat_out[0:1] = jnp.sum(scaled_one, axis=0, keepdims=True)
    stat_out[1:2] = jnp.sum(scaled_one * unit, axis=0, keepdims=True)
    stat_r = wire.spread("row", lambda p: stat_out, lambda p: stat_in.at[me_r])
    stat_in[me_r] = stat_out[...]
    arrived(wide_r)
    wides = slots_of(wide_in)
    term_out[...] = jnp.zeros_like(term_out)
    term_out[0:1] = jnp.sum((grad_one * unit).T, axis=0, keepdims=True)
    term_out[1:2] = jnp.sum(grad_one.T, axis=0, keepdims=True)
    term_out[2:4] = wides
    term_out[4:5] = jnp.sum(mid_cols[own].astype(wide), axis=0, keepdims=True)
    term_out[5:6] = jnp.sum(grad_cols[:, own].astype(wide).T, axis=0, keepdims=True)

    for copy in push_r:
        copy.wait_recv()
    edge = packed.shape[1]
    bands = [matrix[up * edge : (up + 1) * edge] for up in range(3)]
    spots = [(0, 0), (0, 1), (0, 2), (1, 1), (1, 2), (2, 2)]
    for which, (up, across) in enumerate(spots):
        packed[which] = contract(bands[up], bands[across], 1, 1).astype(low)
    packed_s = wire.push(packed.at[rows_at(other, 3)], packed_in, "dp", other)
    packed_s.wait_recv()
    long = 3 * edge
    halved[...] = (
        (packed[rows_at(me_d, 3)].astype(wide) + packed_in[...].astype(wide))
        .astype(low)
        .reshape(long, edge)
    )
    fourth = long // cols
    quarter = rows_at(me_c, fourth)
    quarter_z = wire.spread(
        "col", lambda p: halved.at[rows_at(p, fourth)], lambda p: quarter_in.at[me_c]
    )
    quarter_in[me_c] = halved[quarter]
    term_z = wire.spread("col", lambda p: term_out, lambda p: term_in.at[me_c])
    term_in[me_c] = term_out[...]
    arrived(stat_r)
    stats = slots_of(stat_in) / whole
    input_grad[...] = mid_cols[own].astype(wide).T + inv_one[:, own] * (
        scaled_one - stats[0:1] - unit * stats[1:2]
    )
    arrived(quarter_z)
    gathered[me_d, quarter] = slots_of(quarter_in).astype(low)
    whole_z = wire.spread(
        "col", lambda p: gathered.at[me_d, quarter], lambda p: gathered.at[me_d, quarter]
    )
    whole_s = [wire.push(gathered.at[me_d, quarter], gathered.at[me_d, quarter], "dp", other)]
    arrived(term_z)
    term_pair[me_d] = slots_of(term_in)
    term_s = wire.push(term_pair.at[me_d], term_pair.at[me_d], "dp", other)
    for step in range(1, cols):
        whole_z[step - 1].wait_recv()
        there = rows_at(lax.rem(me_c + cols - step, cols), fourth)
        whole_s.append(
            wire.push(gathered.at[me_d, there], gathered.at[me_d, there], "dp", other)
        )
    arrived(whole_s)
    square = None
    for which, (up, across) in enumerate(spots):
        at = which % 3 * edge
        tile = gathered[which // 3, at : at + edge].astype(wide)
        gram[up * edge : (up + 1) * edge, across * edge : (across + 1) * edge] = tile
        power = jnp.sum(jnp.sum(tile * tile, axis=0, keepdims=True), axis=1, keepdims=True)
        if across > up:
            gram[across * edge : (across + 1) * edge, up * edge : (up + 1) * edge] = tile.T
            power = power + power
        square = power if square is None else square + power
    gram_norm = jnp.sqrt(square) + eps_gram
    now = gram[...] * (1.0 / gram_norm)
    now_low = now.astype(low)
    poly = (coef_b * now + coef_c * contract(now_low, now_low, 1, 0)).astype(low)
    held = coef_a * now + contract(poly, now_low, 1, 0)
    moved = coef_a * matrix[...].astype(wide) + contract(poly, matrix[...], 1, 0)
    now = coef_a * held + contract(held.astype(low), poly, 1, 0)
    now_low = now.astype(low)
    poly = (coef_b * now + coef_c * contract(now_low, now_low, 1, 0)).astype(low)
    moved = coef_a * moved + contract(poly, moved.astype(low), 1, 0)
    ortho[...] = (moved * lax.rsqrt(gram_norm)).astype(low)
    back_r = wire.spread(
        "row", lambda p: ortho.at[rows_at(p, feats)], lambda p: back.at[me_d, me_r]
    )
    back[me_d, me_r] = ortho[rows_at(me_r, feats)]
    back_s = [wire.push(back.at[me_d, me_r], back.at[me_d, me_r], "dp", other)]
    term_s.wait_recv()
    grad_rows[...] = term_pair[0] + term_pair[1]
    arrived(pair)
    for step in range(1, rows):
        back_r[step - 1].wait_recv()
        peer = lax.rem(me_r + rows - step, rows)
        back_s.append(wire.push(back.at[me_d, peer], back.at[me_d, peer], "dp", other))
    arrived(back_s)
    for copy in push_r:
        copy.wait_send()

    @pl.when(giver)
    def _():
        for copy in resid_r:
            copy.wait_send()

    wire.drain()


def last_kernel(rate, vector_rate, *refs):
    wide = jnp.float32
    (
        sum_q, sum_o, sum_f, sum_p, sum_bq, sum_bf, block_in, input_in, rows_in, back,
        w_q, w_o, w_f, w_p, bias_q, bias_f, vectors, mom_q, mom_o, mom_f, mom_p, mom_bq, mom_bf,
        mom_rows,
        block_out, input_grad, grad_q, grad_o, grad_f, grad_p, grad_bq, grad_bf, grad_rows,
        new_q, new_o, new_f, new_p, new_bq, new_bf, new_rows,
        next_q, next_o, next_f, next_p, next_bq, next_bf, next_rows,
    ) = refs
    block_out[...] = block_in[...]
    input_grad[...] = input_in[...]
    share = back.shape[3]
    members = (
        (sum_q, w_q, mom_q, grad_q, new_q, next_q, False),
        (sum_o, w_o, mom_o, grad_o, new_o, next_o, True),
        (sum_f, w_f, mom_f, grad_f, new_f, next_f, False),
        (sum_p, w_p, mom_p, grad_p, new_p, next_p, False),
    )
    for member, (sums, weight, moment, gradient, new, later, flip) in enumerate(members):
        value = sums[0].astype(wide) + sums[1].astype(wide)
        gradient[...] = value
        later[...] = beta_mom * moment[...] + value
        width = weight.shape[1]
        for start in range(0, width, share):
            stop = min(start + share, width)
            turn = back[start // share, member, :, : stop - start].astype(wide)
            if flip:
                turn = turn.T
            here = (slice(None), slice(start, stop))
            new[here] = weight[here].astype(wide) - rate[member] * turn
    vector_members = (
        (sum_bq[0, 0:1] + sum_bq[1, 0:1], bias_q, mom_bq, grad_bq, new_bq, next_bq),
        (sum_bf[0, 0:1] + sum_bf[1, 0:1], bias_f, mom_bf, grad_bf, new_bf, next_bf),
        (rows_in[: vectors.shape[0]], vectors, mom_rows, grad_rows, new_rows, next_rows),
    )
    for value, weight, moment, gradient, new, later in vector_members:
        value = value.reshape(gradient.shape)
        new_moment = beta_mom * moment[...] + value
        gradient[...] = value
        later[...] = new_moment
        new[...] = weight[...] - vector_rate * (value + beta_mom * new_moment)


def paired_local(
    tokens, out_grad, segment_ids, w_qkv, w_out, w_fc, w_proj, bias_qkv, bias_fc, row_vectors,
    mom_qkv, mom_out, mom_fc, mom_proj, mom_bias_qkv, mom_bias_fc, mom_rows,
):
    low, wide = jnp.bfloat16, jnp.float32
    rows, cols = lax.axis_size("row"), lax.axis_size("col")
    block, feats = tokens.shape
    count = block * cols
    piece = block // cols
    width, hidden = w_qkv.shape[1], w_fc.shape[1]
    heads = width // (3 * HD)
    whole = feats * rows
    edge = whole // 3
    share = max(width, hidden, w_out.shape[0]) // 2
    lines = row_vectors.shape[0]
    assert rows == 4 and w_out.shape[0] <= share < width <= 2 * share
    shape = jax.ShapeDtypeStruct
    loose = pl.BlockSpec(memory_space=pl.ANY)
    near = pl.BlockSpec(memory_space=pltpu.VMEM)
    outs = [
        shape((2, feats, width), low),
        shape((2, w_out.shape[0], feats), low),
        shape((2, feats, hidden), low),
        shape((2, feats, hidden), low),
        shape((2, 8, width), wide),
        shape((2, 8, hidden), wide),
        shape((feats, block), low),
        shape((feats, block), wide),
        shape((8, feats), wide),
        shape((2, rows, feats, share), low),
    ]
    buffers = [
        ((rows, feats, count), low),
        ((feats, count), low),
        ((rows, feats, block), low),
        ((rows, block, feats), low),
        ((rows, lines, feats), wide),
        ((feats, width), low),
        ((rows, width, feats), low),
        ((cols, rows, w_out.shape[0], feats), low),
        ((rows, feats, hidden), low),
        ((rows, feats, hidden), low),
        ((rows, feats, count), low),
        ((width, count), low),
        ((width, 1), wide),
        ((rows, 2, feats, 1), wide),
        ((count, count), wide),
        ((heads, count, count), wide),
        ((heads * HD, count), low),
        ((cols, heads * HD, block), low),
        ((rows, block, feats), wide),
        ((block, 1), wide),
        ((rows, block, feats), low),
        ((count, feats), low),
        ((rows, block, feats), wide),
        ((block, feats), wide),
        ((count, hidden), low),
        ((count, hidden), low),
        ((rows, block, feats), low),
        ((cols, rows, piece, feats), low),
        ((rows, piece, feats), low),
        ((rows, block, feats), low),
        ((count, feats), low),
        ((heads * HD, count), low),
        ((width, count), low),
        ((HD, count), wide),
        ((HD, count), wide),
        ((1, count), wide),
        ((1, count), wide),
        ((rows, 2, feats), wide),
        ((rows, 2, feats), wide),
        ((feats, count), low),
        ((cols, feats, block), low),
        ((feats, count), low),
        ((cols, feats, block), low),
        ((2, block), wide),
        ((rows, 2, block), wide),
        ((8, feats), wide),
        ((cols, 8, feats), wide),
        ((2, 8, feats), wide),
        (mom_qkv.shape, wide),
        (mom_out.shape, wide),
        (mom_fc.shape, wide),
        (mom_proj.shape[::-1], wide),
        ((rows, feats, 2 * share), low),
        ((whole, share), low),
        ((6, edge, edge), low),
        ((3, edge, edge), low),
        ((whole, edge), low),
        ((cols, whole // cols, edge), low),
        ((2, whole, edge), low),
        ((whole, whole), wide),
        ((whole, share), low),
    ]
    middle = pl.pallas_call(
        step_kernel,
        out_shape=outs,
        in_specs=[loose, loose, near, loose, loose, loose, loose, near, near] + [loose] * 5,
        out_specs=[near] * len(outs),
        scratch_shapes=[pltpu.VMEM(size, kind) for size, kind in buffers]
        + [
            pltpu.SemaphoreType.DMA((step_wires,)),
            pltpu.SemaphoreType.DMA((step_wires,)),
            pltpu.SemaphoreType.DMA((11,)),
        ],
        compiler_params=pltpu.CompilerParams(collective_id=20, has_side_effects=True),
    )(
        tokens.T,
        out_grad.T,
        segment_ids,
        w_qkv,
        w_out,
        w_fc,
        w_proj.T,
        bias_qkv[None],
        bias_fc[None],
        row_vectors,
        mom_qkv,
        mom_out,
        mom_fc,
        mom_proj.T,
    )
    longest = [
        max(whole, width * cols),
        max(whole, w_out.shape[0] * cols),
        max(whole, hidden * cols),
        max(whole, hidden * cols),
    ]
    rate = tuple(rate_matrix * math.sqrt(size) for size in longest)
    matrices = [w_qkv.shape, w_out.shape, w_fc.shape, w_proj.shape[::-1]]
    vectors = [bias_qkv.shape, bias_fc.shape, row_vectors.shape]
    group = [shape(size, wide) for size in matrices + vectors]
    results = list(
        pl.pallas_call(
            functools.partial(last_kernel, rate, rate_vector / math.sqrt(count * 2)),
            out_shape=[shape((feats, block), low), shape((feats, block), wide)] + group * 3,
            in_specs=[near] * 24,
            out_specs=[near] * 23,
        )(
            *middle,
            w_qkv,
            w_out,
            w_fc,
            w_proj.T,
            bias_qkv,
            bias_fc,
            row_vectors,
            mom_qkv,
            mom_out,
            mom_fc,
            mom_proj.T,
            mom_bias_qkv,
            mom_bias_fc,
            mom_rows,
        )
    )
    for which in (0, 1, 5, 12, 19):
        results[which] = results[which].T
    return tuple(results)


def local(
    tokens,
    out_grad,
    segment_ids,
    w_qkv,
    w_out,
    w_fc,
    w_proj,
    bias_qkv,
    bias_fc,
    row_vectors,
    mom_qkv,
    mom_out,
    mom_fc,
    mom_proj,
    mom_bias_qkv,
    mom_bias_fc,
    mom_rows,
):
    low = jnp.bfloat16
    score_scale = 1.0 / math.sqrt(HD)
    row_parts = lax.axis_size("row")
    col_parts = lax.axis_size("col")
    dp_parts = lax.axis_size("dp")
    own_tokens, own_features = tokens.shape
    token_count = own_tokens * col_parts
    feature_count = own_features * row_parts
    token_base = lax.axis_index("col") * own_tokens
    feature_base = lax.axis_index("row") * own_features

    def own_columns(whole):
        return lax.dynamic_slice_in_dim(whole, feature_base, own_features, 1)

    def own_block(whole):
        return lax.dynamic_slice(whole, (token_base, feature_base), (own_tokens, own_features))

    def own_rows(whole):
        return lax.dynamic_slice_in_dim(whole, token_base, own_tokens, 0)

    proj_flip = w_proj.T
    tokens_tall, grad_tall, out_tall = exchange(
        "col", [tokens, out_grad, w_out.T], [False] * 3, 0
    )
    grad_cols = grad_tall.reshape(token_count, own_features)
    matrices = [w_qkv, side_by_side(out_tall), w_fc, proj_flip]
    halved = dp_parts == 2
    pieces = matrices
    if halved:
        piece_size = own_features // 2
        pieces = [
            lax.dynamic_slice_in_dim(whole, lax.axis_index("dp") * piece_size, piece_size, 0)
            for whole in matrices
        ]
    token_slots, grad_slots, vector_slots, *gathered = exchange(
        "row",
        [
            tokens_tall.reshape(token_count, own_features),
            grad_cols.reshape(row_parts, -1, own_features),
            row_vectors,
        ]
        + pieces,
        [False, True, False] + [False] * 4,
        1,
    )
    if halved:
        gathered = [
            both.transpose(1, 0, 2, 3)
            for both in exchange("dp", gathered, [False] * 4, 19)
        ]
    qkv_cols, out_flip, fc_cols, proj_cols = [
        slots.reshape(feature_count, -1) for slots in gathered
    ]
    tokens_all = side_by_side(token_slots)
    grad_part = side_by_side(grad_slots)
    vectors_all = side_by_side(vector_slots)
    gain_one, shift_one, gain_two, shift_two, bias_out, _ = [
        vectors_all[which] for which in range(6)
    ]

    resid_in = tokens_all.astype(jnp.float32)
    mean_one, inv_one = norm_stats(resid_in)
    unit_one = (resid_in - mean_one) * inv_one
    act_one = (unit_one * gain_one + shift_one).astype(low)
    qkv_local = (product(act_one, qkv_cols, False) + bias_qkv).astype(low)
    heads_local = qkv_local.shape[1] // (3 * HD)
    qkv_tiles = qkv_local.reshape(token_count, heads_local, 3, HD).transpose(2, 1, 0, 3)
    query, key, value = qkv_tiles[0], qkv_tiles[1], qkv_tiles[2]
    segment_row = segment_ids[0]
    positions = jnp.arange(token_count, dtype=jnp.int32)
    allowed = (positions[None, :] <= positions[:, None]) & (
        segment_row[None, :] == segment_row[:, None]
    )
    scores = (
        jnp.einsum("hqe,hke->hqk", query, key, preferred_element_type=jnp.float32) * score_scale
    )
    scores = jnp.where(allowed[None], scores, -jnp.inf)
    row_max = jnp.max(scores, axis=2, keepdims=True)
    raised = jnp.exp(scores - row_max)
    probs = raised / jnp.sum(raised, axis=2, keepdims=True)
    prob_low = probs.astype(low)
    attended = jnp.einsum(
        "hqk,hke->hqe", prob_low, value, preferred_element_type=jnp.float32
    ).astype(low)
    attn_local = attended.transpose(1, 0, 2).reshape(token_count, heads_local * HD)
    part_tokens = token_count // row_parts
    part_base = lax.axis_index("row") * part_tokens

    def part_rows(whole):
        return lax.dynamic_slice_in_dim(whole, part_base, part_tokens, 0)

    (attn_slots,) = exchange("col", [part_rows(attn_local)], [False], 2)
    attn_part = jnp.concatenate([attn_slots[part] for part in range(col_parts)], axis=1)
    resid_mid = part_rows(resid_in) + product(attn_part, out_flip, True) + bias_out
    mean_two, inv_two = norm_stats(resid_mid)
    unit_two = (resid_mid - mean_two) * inv_two
    act_two = (unit_two * gain_two + shift_two).astype(low)
    hidden_pre = product(act_two, fc_cols, False) + bias_fc
    hidden = gelu_value(hidden_pre).astype(low)
    grad_hidden = product(grad_part, proj_cols, False)
    grad_pre = (gelu_slope(hidden_pre) * grad_hidden).astype(low)

    piece_tokens = part_tokens // col_parts
    piece_base = lax.axis_index("col") * piece_tokens

    def piece_rows(part):
        return lax.dynamic_slice_in_dim(part, piece_base, piece_tokens, 0)

    (two_slots,) = exchange(
        "col",
        [product(grad_pre, fc_cols, True).astype(low).reshape(col_parts, piece_tokens, -1)],
        [True],
        3,
    )
    grad_norm_two = total(two_slots)
    unit_two_piece = piece_rows(unit_two)
    scaled = grad_norm_two * gain_two
    first_mean = jnp.mean(scaled, axis=1, keepdims=True)
    second_mean = jnp.mean(scaled * unit_two_piece, axis=1, keepdims=True)
    grad_mid_piece = piece_rows(grad_part).astype(jnp.float32) + piece_rows(inv_two) * (
        scaled - first_mean - unit_two_piece * second_mean
    )
    grad_mid_low = grad_mid_piece.astype(low)
    (mid_slots,) = exchange("col", [grad_mid_low], [False], 4)
    mid_part = mid_slots.reshape(part_tokens, feature_count)
    out_rows = lax.dynamic_slice_in_dim(
        out_flip, lax.axis_index("col") * w_out.shape[0], w_out.shape[0], 1
    )
    grad_attn_part = product(mid_part, out_rows, False).astype(low)
    split = lambda rows: rows.reshape(part_tokens, row_parts, own_features).transpose(1, 0, 2)
    attn_grad_slots, mid_cols, act_two_cols, hidden_slots, grad_pre_slots, resid_cols = exchange(
        "row",
        [
            grad_attn_part,
            split(mid_part),
            split(act_two),
            hidden,
            grad_pre,
            split(resid_mid),
        ],
        [False, True, True, False, False, True],
        5,
    )
    grad_attn = (
        attn_grad_slots.reshape(token_count, heads_local, HD).transpose(1, 0, 2)
    )
    mid_cols = mid_cols.reshape(token_count, own_features)
    act_two_cols = act_two_cols.reshape(token_count, own_features)
    resid_cols = resid_cols.reshape(token_count, own_features)
    hidden_all = hidden_slots.reshape(token_count, -1)
    grad_pre_all = grad_pre_slots.reshape(token_count, -1)

    grad_value = jnp.einsum(
        "hqk,hqe->hke", prob_low, grad_attn, preferred_element_type=jnp.float32
    )
    grad_probs = jnp.einsum("hqe,hke->hqk", grad_attn, value, preferred_element_type=jnp.float32)
    row_dot = jnp.sum(
        grad_attn.astype(jnp.float32) * attended.astype(jnp.float32), axis=2, keepdims=True
    )
    grad_scores = (score_scale * probs * (grad_probs - row_dot)).astype(low)
    grad_query = jnp.einsum("hqk,hke->hqe", grad_scores, key, preferred_element_type=jnp.float32)
    grad_key = jnp.einsum("hqk,hqe->hke", grad_scores, query, preferred_element_type=jnp.float32)
    grad_qkv_low = (
        jnp.stack([grad_query.astype(low), grad_key.astype(low), grad_value.astype(low)], axis=0)
        .transpose(2, 1, 0, 3)
        .reshape(token_count, heads_local * 3 * HD)
    )

    grad_blocks = (
        inner_rows(own_columns(act_one), grad_qkv_low),
        inner_rows(attn_local, mid_cols),
        inner_rows(act_two_cols, grad_pre_all),
        inner_rows(hidden_all, grad_cols),
    )
    bias_blocks = jnp.concatenate(
        [
            jnp.sum(grad_qkv_low, axis=0, dtype=jnp.float32),
            jnp.sum(grad_pre_all, axis=0, dtype=jnp.float32),
        ]
    )[None]
    if dp_parts == 2:
        group_slots = exchange(
            "dp", [block.astype(low) for block in grad_blocks] + [bias_blocks], [False] * 5, 6
        )
        summed = [total(slots) for slots in group_slots]
    else:
        summed = [lax.psum(block.astype(low), "dp").astype(jnp.float32) for block in grad_blocks]
        summed.append(lax.psum(bias_blocks, "dp"))
    bias_sums = summed.pop()[0]
    summed = summed + [bias_sums[: bias_qkv.shape[0]], bias_sums[bias_qkv.shape[0] :]]

    weights = (w_qkv, w_out, w_fc, w_proj)
    moments = (mom_qkv, mom_out, mom_fc, mom_proj)
    flips = (False, True, False, True)
    new_moms = [beta_mom * moments[member] + summed[member] for member in range(4)]
    pushes = [
        (summed[member] + beta_mom * new_moms[member]).astype(low) for member in range(4)
    ]
    upright = [pushes[member].T if flips[member] else pushes[member] for member in range(4)]
    widest = max(piece.shape[1] for piece in upright)
    share = -(-widest // dp_parts)
    assert row_parts == len(upright)
    outgoing = jnp.stack(
        [
            jnp.pad(piece, ((0, 0), (0, share * dp_parts - piece.shape[1])))
            for piece in upright
        ]
    )
    outgoing = lax.dynamic_slice_in_dim(outgoing, lax.axis_index("dp") * share, share, 2)
    outward = product(hidden_all, proj_flip, True).astype(low)
    inward = product(grad_qkv_low, w_qkv, True).astype(low)
    arrived, block_slots, one_slots = exchange(
        ["row", "col", "col"],
        [
            outgoing,
            outward.reshape(col_parts, own_tokens, own_features),
            inward.reshape(col_parts, own_tokens, own_features),
        ],
        [True] * 3,
        7,
    )
    matrix = arrived.reshape(feature_count, share)
    gram_low = product(matrix, matrix, True).astype(low)
    edge = feature_count // 3
    spots = [(0, 0), (0, 1), (0, 2), (1, 1), (1, 2), (2, 2)]
    packed = jnp.concatenate(
        [
            gram_low[up * edge : (up + 1) * edge, across * edge : (across + 1) * edge]
            for up, across in spots
        ],
        axis=0,
    )
    block_out = (own_rows(resid_cols) + total(block_slots) + row_vectors[5]).astype(low)
    grad_norm_one = total(one_slots)
    unit_one_own = own_block(unit_one)
    scaled_one = grad_norm_one * row_vectors[0]
    stat_pair = jnp.stack(
        [jnp.sum(scaled_one, axis=1), jnp.sum(scaled_one * unit_one_own, axis=1)]
    )
    wide_terms = jnp.stack(
        [
            jnp.sum(grad_norm_two * unit_two_piece, axis=0),
            jnp.sum(grad_norm_two, axis=0),
        ]
    )
    wide_slot_terms = wide_terms.reshape(2, row_parts, own_features).transpose(1, 0, 2)
    if dp_parts == 2:
        stat_slots, wide_slots, half_slots = exchange(
            ["row", "row", "dp"],
            [stat_pair, wide_slot_terms, packed.reshape(dp_parts, -1, edge)],
            [False, True, True],
            8,
        )
        gram_half = total(half_slots).astype(low)
    else:
        stat_slots, wide_slots = exchange(
            "row", [stat_pair, wide_slot_terms], [False, True], 8
        )
        gram_half = lax.psum(packed, "dp")
    stat_sum = total(stat_slots)
    first_sum, second_sum = stat_sum[0][:, None], stat_sum[1][:, None]
    wide_sum = total(wide_slots)
    input_grad = own_rows(mid_cols).astype(jnp.float32) + own_rows(inv_one) * (
        scaled_one - first_sum / feature_count - unit_one_own * (second_sum / feature_count)
    )
    row_terms = jnp.stack(
        [
            jnp.sum(grad_norm_one * unit_one_own, axis=0),
            jnp.sum(grad_norm_one, axis=0),
            wide_sum[0],
            wide_sum[1],
            jnp.sum(own_rows(mid_cols), axis=0, dtype=jnp.float32),
            jnp.sum(out_grad, axis=0, dtype=jnp.float32),
        ]
    )
    quarter_slots, term_slots = exchange(
        "col",
        [gram_half.reshape(col_parts, -1, edge), row_terms],
        [True, False],
        9,
    )
    (whole_slots,) = exchange("col", [total(quarter_slots).astype(low)], [False], 10)
    gram_half = whole_slots.reshape(gram_half.shape)
    if dp_parts == 2:
        gram_slots, pair_slots = exchange(
            "dp", [gram_half, total(term_slots)], [False, False], 11
        )
        gram_half = gram_slots
    else:
        (pair_slots,) = exchange("dp", [total(term_slots)], [False], 11)
    grad_rows = total(pair_slots)
    tiles = gram_half.reshape(len(spots), edge, edge)
    found = {spot: tiles[which] for which, spot in enumerate(spots)}
    gram = jnp.concatenate(
        [
            jnp.concatenate(
                [
                    found[up, across] if across >= up else found[across, up].T
                    for across in range(3)
                ],
                axis=1,
            )
            for up in range(3)
        ],
        axis=0,
    ).astype(jnp.float32)
    factor, scale, gram_norm = polynomial_factor(gram)
    ortho = (scale * matrix.astype(jnp.float32) + matrix_product(factor, matrix)) * lax.rsqrt(
        gram_norm
    )
    (back,) = exchange(
        "row", [ortho.astype(low).reshape(row_parts, own_features, share)], [True], 12
    )
    if dp_parts == 2:
        (ortho_slots,) = exchange("dp", [back], [False], 13)
        orthos = jnp.concatenate([ortho_slots[part] for part in range(dp_parts)], axis=2)
    else:
        orthos = lax.all_gather(back, "dp", axis=2, tiled=True)
    new_weights = []
    for member in range(4):
        piece = orthos[member, :, : upright[member].shape[1]]
        if flips[member]:
            piece = piece.T
        longest = max(
            upright[member].shape[0] * row_parts, upright[member].shape[1] * col_parts
        )
        new_weights.append(
            weights[member].astype(jnp.float32)
            - rate_matrix * math.sqrt(longest) * piece.astype(jnp.float32)
        )

    vector_rate = rate_vector / math.sqrt(token_count * dp_parts)

    def vector_step(weight, gradient, moment):
        new_moment = beta_mom * moment + gradient
        return (weight - vector_rate * (gradient + beta_mom * new_moment), new_moment)

    new_bias_qkv, new_mom_bias_qkv = vector_step(bias_qkv, summed[4], mom_bias_qkv)
    new_bias_fc, new_mom_bias_fc = vector_step(bias_fc, summed[5], mom_bias_fc)
    new_rows, new_mom_rows = vector_step(row_vectors, grad_rows, mom_rows)
    return (
        block_out,
        input_grad,
        summed[0],
        summed[1],
        summed[2],
        summed[3],
        summed[4],
        summed[5],
        grad_rows,
        new_weights[0],
        new_weights[1],
        new_weights[2],
        new_weights[3],
        new_bias_qkv,
        new_bias_fc,
        new_rows,
        new_moms[0],
        new_moms[1],
        new_moms[2],
        new_moms[3],
        new_mom_bias_qkv,
        new_mom_bias_fc,
        new_mom_rows,
    )


def solution(mesh):
    placed = (
        P(("dp", "col"), "row"),
        P(("dp", "col"), "row"),
        P("dp", None),
        P("row", "col"),
        P("col", "row"),
        P("row", "col"),
        P("col", "row"),
        P("col"),
        P("col"),
        P(None, "row"),
        P("row", "col"),
        P("col", "row"),
        P("row", "col"),
        P("col", "row"),
        P("col"),
        P("col"),
        P(None, "row"),
    )
    return jax.shard_map(
        paired_local if mesh.shape["dp"] == 2 else local,
        mesh=mesh,
        in_specs=placed,
        out_specs=(
            P(("dp", "col"), "row"),
            P(("dp", "col"), "row"),
            P("row", "col"),
            P("col", "row"),
            P("row", "col"),
            P("col", "row"),
            P("col"),
            P("col"),
            P(None, "row"),
            P("row", "col"),
            P("col", "row"),
            P("row", "col"),
            P("col", "row"),
            P("col"),
            P("col"),
            P(None, "row"),
            P("row", "col"),
            P("col", "row"),
            P("row", "col"),
            P("col", "row"),
            P("col"),
            P("col"),
            P(None, "row"),
        ),
        check_vma=False,
    )
```
